128 devices in a mesh: depth: 4 (over y_lo, core), strips: 32 (over z, y_hi, x).
Axes of the slice: x: 4, y: 4 (y_hi: 2, y_lo: 2; y = y_hi * 2 + y_lo), z: 4, core: 2. Of those that a mesh axis runs over, the one named last changes fastest.
Arguments:
- pressure: float32 [32, 4096, 1024], P('depth', 'strips'), may hold values from -3 to 3
- texture: int32 [32, 4096, 1024], P('depth', 'strips'), may hold values from 0 to 11
- active: int32 [32, 4096, 1024], P('depth', 'strips'), may hold values 0 or 1
- rain: float32 [4096, 1024], P('strips'), may hold values from 0 to 40
- k_sat: float32 [12], replicated, may hold values from 0.05 to 2
- alpha: float32 [12], replicated, may hold values from 0.5 to 4
- theta_sat: float32 [12], replicated, may hold values from 0.35 to 0.5
- head_old: float32 [4096, 1024], P('strips', 'depth'), may hold values from -4 to 4
- cell_code: int32 [4096, 1024], P('strips', 'depth'), may hold values from 0 to 2
- section: float32 [4096, 1024], P('strips', 'depth'), may hold values from -4 to 4
Outputs:
- moisture_new: float32 [32, 4096, 1024], P('depth', 'strips')
- head: float32 [4096, 1024], P('strips', 'depth')
The draws below stay inside these ranges and needn't reach their ends.
All inputs are finite; a program needn't handle non-finite values. No bound on the sum of `active` on one device may be relied on, other than what follows from the above.
Results may differ from the reference program's by a relative error of at most 0.00002.
Values sent between devices are 32-bit elements; how exact they have to be, the bound alone decides.
A program may use at most 128 MiB of HBM per device.

```python
import math
import jax
import jax.numpy as jnp
from jax import lax

NCLASS = 12
SWEEPS = 3
LAYERS = 32
NX = 4096
NY = 1024


def plant(values, rng, smallest, high):
    longest = values.shape.index(max(values.shape))
    spots = []
    for shift in (0, 1):
        where = [jax.random.randint(jax.random.fold_in(rng, axis), (), 0, length) for axis, length in enumerate(values.shape)]
        where[longest] = (where[longest] + shift) % values.shape[longest]
        spots.append(tuple(where))
    return values.at[spots[0]].set(smallest).at[spots[1]].set(high)


def levels(stream_key, shape, cuts, least, high):
    loudness = 1.0
    for dim, blocks in cuts:
        steps = jax.random.uniform(jax.random.fold_in(jax.random.fold_in(stream_key, 6), dim), (blocks,), jnp.float32, least / len(cuts), high / len(cuts))
        loudness = loudness * jnp.repeat(jnp.exp(steps), shape[dim] // blocks).reshape((-1,) + (1,) * (len(shape) - 1 - dim))
    return loudness


def centred(own_key, extent, spread, most, shards=(), kind=jnp.bfloat16):
    drawn = jax.random.normal(own_key, extent, jnp.float32) * spread
    if len(shards) > 0:
        drawn = levels(own_key, extent, shards, -0.22, 0.18) * drawn
    return jnp.clip(drawn, min=-most, max=most).astype(kind)


def setup_inputs(seed: int = 0) -> dict:
    keys = jax.random.split(jax.random.key(seed), 11)
    pressure = centred(keys[0], (LAYERS, NX, NY), 0.5, 3.0, ((0, 4), (1, 32)), jnp.float32)
    texture = plant(jax.random.randint(keys[1], (LAYERS, NX, NY), 0, NCLASS), jax.random.fold_in(keys[1], 1), 0, NCLASS - 1).astype(jnp.int32)
    active = plant((jax.random.randint(keys[2], (LAYERS, NX, NY), 0, 8) < 7).astype(jnp.int32), jax.random.fold_in(keys[2], 1), 0, 1)
    rain = jnp.clip(40.0 * jax.random.uniform(keys[3], (NX, NY), jnp.float32) ** levels(keys[3], (NX, NY), ((0, 32),), -0.2, 0.2), 0.0, 40.0)
    k_sat = jnp.clip(jnp.exp(jax.random.uniform(keys[4], (NCLASS,), jnp.float32, math.log(0.05), math.log(2.0))), 0.05, 2.0)
    alpha = jnp.clip(jnp.exp(jax.random.uniform(keys[5], (NCLASS,), jnp.float32, math.log(0.5), math.log(4.0))), 0.5, 4.0)
    theta_sat = jnp.clip(jax.random.uniform(keys[6], (NCLASS,), jnp.float32, 0.35, 0.5), 0.35, 0.5)
    head_old = centred(keys[7], (NX, NY), 1.0, 4.0, ((0, 32), (1, 4)), jnp.float32)
    cell_code = plant(jax.random.randint(keys[8], (NX, NY), 0, 3), jax.random.fold_in(keys[8], 1), 0, 2).astype(jnp.int32)
    section = centred(keys[9], (NX, NY), 1.0, 4.0, ((0, 32), (1, 4)), jnp.float32)
    return {"pressure": pressure, "texture": texture, "active": active, "rain": rain, "k_sat": k_sat, "alpha": alpha, "theta_sat": theta_sat, "head_old": head_old, "cell_code": cell_code, "section": section}


layer_thick = 0.05
soil_step = 0.0002
spec_yield = 0.02
leak_rate = 0.5
river_cond = 0.5
fixed_cond = 3.0

def lookup(texture, table):
    result = jnp.zeros(texture.shape, jnp.float32)
    for class_id in range(table.shape[0]):
        result = result + jnp.where(texture == class_id, table[class_id], jnp.float32(0.0))
    return result

def face_flux(psi_up, cond_up, psi_low, cond_low):
    return 0.5 * (cond_up + cond_low) * ((psi_up - psi_low) / layer_thick + 1.0)

def neighbour(padded, shift_a, shift_b):
    return padded[1 + shift_a:padded.shape[0] - 1 + shift_a, 1 + shift_b:padded.shape[1] - 1 + shift_b]

def sweep(head_pad, trans_pad, base, rhs):
    centre = neighbour(trans_pad, 0, 0)
    total = base
    accum = rhs
    for shift_a, shift_b in ((1, 0), (-1, 0), (0, 1), (0, -1)):
        face = jnp.sqrt(centre * neighbour(trans_pad, shift_a, shift_b))
        accum = accum + face * neighbour(head_pad, shift_a, shift_b)
        total = total + face
    return accum / total

def reference(pressure, texture, active, rain, k_sat, alpha, theta_sat, head_old, cell_code, section):
    sat_cond = lookup(texture, k_sat)
    shape_par = lookup(texture, alpha)
    porous = lookup(texture, theta_sat)
    suction = jnp.minimum(pressure, 0.0)
    wetness = jnp.exp(0.5 * shape_par * suction)
    conduct = sat_cond * jnp.exp(shape_par * suction) * active.astype(jnp.float32)
    moisture = porous * (0.15 + 0.85 * wetness)
    trans = lax.optimization_barrier(jnp.sum(conduct, axis=0)) * layer_thick
    store = spec_yield + lax.optimization_barrier(jnp.sum(0.85 * porous * (1.0 - wetness), axis=0)) * layer_thick
    recharge = leak_rate * (lax.optimization_barrier(jnp.sum(conduct * wetness, axis=0)) * layer_thick)
    river = jnp.where(cell_code == 1, jnp.float32(river_cond), jnp.where(cell_code == 2, jnp.float32(fixed_cond), jnp.float32(0.0)))
    base = store + river
    rhs = store * head_old + recharge + river * section
    head = head_old
    trans_pad = jnp.pad(trans, 1)
    for sweep_id in range(SWEEPS):
        head = sweep(jnp.pad(head, 1), trans_pad, base, rhs)
    inner = face_flux(pressure[:-1], conduct[:-1], pressure[1:], conduct[1:])
    bottom = conduct[-1] * ((pressure[-1] - head) / (0.5 * layer_thick) + 1.0)
    lower = jnp.concatenate([inner, bottom[None]], axis=0)
    upper = jnp.concatenate([rain[None], inner], axis=0)
    moisture_new = moisture + soil_step / layer_thick * (upper - lower)
    return (moisture_new, head)
```

```python
import functools
import math

import jax
import jax.numpy as jnp
from jax import lax
from jax.experimental import pallas as pl
from jax.experimental.pallas import tpu as pltpu
from jax.sharding import PartitionSpec as P

MESH = pl.DeviceIdType.MESH
SWEEPS = 3

layer_thick = 0.05
soil_step = 0.0002
spec_yield = 0.02
leak_rate = 0.5
river_cond = 0.5
fixed_cond = 3.0
face_scale = soil_step / layer_thick

R = 16
RE = 32
PAD = 16
LANES = 128


def pick(table, index):
    dims = lax.GatherDimensionNumbers(
        offset_dims=(),
        collapsed_slice_dims=(0,),
        start_index_map=(0,),
        operand_batching_dims=(1,),
        start_indices_batching_dims=(1,),
    )
    rows = [
        lax.gather(
            table,
            index[8 * i : 8 * i + 8, :, None],
            dims,
            slice_sizes=(1, 1),
            mode=lax.GatherScatterMode.PROMISE_IN_BOUNDS,
        )
        for i in range(index.shape[0] // 8)
    ]
    return jnp.concatenate(rows, axis=0)


def flux(psi_up, cond_up, psi_low, cond_low):
    return (cond_up + cond_low) * (
        (psi_up - psi_low) * (0.5 * face_scale / layer_thick) + 0.5 * face_scale
    )


def kernel(
    strips, ks, al, th, p_hbm, t_hbm, a_hbm, rain_hbm, h_hbm, code_hbm, sec_hbm,
    moist, head,
    pbuf, tbuf, abuf, rain, h0, code, sec, tabs, part, recv1, xs, recv2, c0, c7,
    dn_p, dn_c, up_p, up_c, fb_out, fb_in, fa_out, fa_in,
    E, H, C, colsend, colrecv, heads,
    load_sem, misc_sem, s1_send, s1_recv, s2_send, s2_recv,
    face_send, face_recv, col_send, col_recv, row_send, row_recv, head_send, head_recv,
):
    layers, rows_all, cols_all = pbuf.shape
    chunks, edges = rows_all // R, rows_all // RE
    tile = h0.shape[1]
    wide = tile + 2 * LANES
    cols_a = dn_p.shape[1]
    part_a, part_b = pl.ds(0, cols_a), pl.ds(cols_a, cols_all - cols_a)
    body = pl.ds(PAD, rows_all)
    mid = pl.ds(LANES, tile)
    last = layers - 1
    depth, strip = lax.axis_index("depth"), lax.axis_index("strips")
    core, chip = depth % 2, depth // 2
    mate = {"depth": chip * 2 + 1 - core}
    cross = {"depth": (depth + 2) % 4}
    above, below = {"depth": depth - 1}, {"depth": depth + 1}
    north, south = {"strips": strip - 1}, {"strips": strip + 1}
    has_up, has_down = depth > 0, depth < 3
    has_north, has_south = strip > 0, strip < strips - 1

    def remote(src, dst, send, recv, device):
        return pltpu.make_async_remote_copy(
            src_ref=src, dst_ref=dst, send_sem=send, recv_sem=recv,
            device_id=device, device_id_type=MESH,
        )

    barrier = pltpu.get_barrier_semaphore()

    def greet(device):
        pl.semaphore_signal(barrier, inc=1, device_id=device, device_id_type=MESH)

    for step in (1, 2, 3):
        greet({"depth": (depth + step) % 4})
    pl.when(has_north)(lambda: greet(north))
    pl.when(has_south)(lambda: greet(south))

    def load(which, chunk):
        src, dst = ((p_hbm, pbuf), (t_hbm, tbuf), (a_hbm, abuf))[which]
        where = pl.ds(pl.multiple_of(chunk * R, R), R)
        return pltpu.make_async_copy(src.at[:, where, :], dst.at[:, where, :], load_sem.at[which, chunk])

    small = [
        pltpu.make_async_copy(src, dst, misc_sem.at[i])
        for i, (src, dst) in enumerate(((h_hbm, h0), (code_hbm, code), (sec_hbm, sec), (rain_hbm, rain)))
    ]
    for i in range(chunks):
        for which in range(3):
            load(which, (i + chunks - 1) % chunks).start()
    for copy in small:
        copy.start()

    scales = (1.0, 0.5 * math.log2(math.e), 0.85)
    row = lax.broadcasted_iota(jnp.int32, (8, LANES), 0)
    for i, (ref, scale) in enumerate(zip((ks, al, th), scales)):
        low = high = jnp.zeros((8, LANES), jnp.float32)
        for c in range(ref.shape[0]):
            value = ref[c] * scale
            if c < 8:
                low = jnp.where(row == c, value, low)
            else:
                high = jnp.where(row == c - 8, value, high)
        tabs[i, 0] = low
        tabs[i, 1] = high

    def blank(first, count):
        for q in range(4):
            E[q, first : first + count, :] = jnp.full((count, wide), 1.0 if q == 1 else 0.0, jnp.float32)

    blank(0, 8)
    blank(PAD + rows_all + 8, 8)
    pl.when(strip == 0)(lambda: blank(8, 8))
    pl.when(strip == strips - 1)(lambda: blank(PAD + rows_all, 8))
    for side in range(2):
        H[side, 0:8, :] = jnp.zeros((8, wide), jnp.float32)
        H[side, 2 * PAD + rows_all - 8 :, :] = jnp.zeros((8, wide), jnp.float32)

    def stage1(chunk):
        return remote(
            part.at[chunk, 1 - core], recv1.at[chunk], s1_send.at[chunk], s1_recv.at[chunk], mate
        )

    def stage2(chunk):
        return remote(xs.at[chunk], recv2.at[chunk], s2_send.at[chunk], s2_recv.at[chunk], cross)

    def column_pass(chunk):
        for which in range(3):
            load(which, chunk).wait()
        where = pl.ds(pl.multiple_of(chunk * R, R), R)

        def lane_tile(block, half):
            cols = pl.ds(pl.multiple_of(block * tile + half * LANES, LANES), LANES)
            total = None
            for k in range(layers):
                p, t, a = pbuf[k, where, cols], tbuf[k, where, cols], abuf[k, where, cols]
                index, upper = t & 7, t >= 8
                sat, shape, pore = (
                    jnp.where(upper, pick(tabs[i, 1], index), pick(tabs[i, 0], index)) for i in range(3)
                )
                wet = jnp.exp2(shape * jnp.minimum(p, 0.0))
                cond = sat * (wet * wet) * a.astype(jnp.float32)
                dry = pore * (1.0 - wet)
                water = pore * (1.0 / 0.85) - dry
                charge = cond * wet
                if k == 0:
                    c0[where, cols] = cond
                    total = (cond, dry, charge)
                else:
                    total = (total[0] + cond, total[1] + dry, total[2] + charge)
                    inner = flux(p_up, cond_up, p, cond)
                    moist[k - 1, where, cols] = water_up - inner
                    water = water + inner
                p_up, cond_up, water_up = p, cond, water
            moist[last, where, cols] = water_up
            c7[where, cols] = cond_up
            for q in range(3):
                part[chunk, block % 2, block // 2, q, :, half * LANES : (half + 1) * LANES] = total[q]

        @pl.loop(0, cols_all // tile)
        def _(block):
            for half in range(tile // LANES):
                lane_tile(block, half)

    @pl.loop(0, chunks + 1)
    def _(i):
        @pl.when(i < chunks)
        def _():
            column_pass((i + chunks - 1) % chunks)

        @pl.when(i == 0)
        def _():
            pl.semaphore_wait(barrier, 3 + (strip + strips - 1) // strips + (2 * strips - 2 - strip) // strips)

        @pl.when(i < chunks)
        def _():
            stage1((i + chunks - 1) % chunks).start()

        @pl.when(i > 0)
        def _():
            chunk = (i + chunks - 2) % chunks
            stage1(chunk).wait_recv()
            xs[chunk] = part[chunk, core, 1 - chip] + recv1[chunk, 1 - chip]
            stage2(chunk).start()

    def face(kind, e):
        where = pl.ds(pl.multiple_of(e * RE, RE), RE)
        src, dst, device = (
            (pbuf.at[last, where, part_a], dn_p.at[where], below),
            (c7.at[where, part_a], dn_c.at[where], below),
            (pbuf.at[0, where, part_b], up_p.at[where], above),
            (c0.at[where, part_b], up_c.at[where], above),
            (fb_out.at[where], fb_in.at[where], below),
            (fa_out.at[where], fa_in.at[where], above),
        )[kind]
        return remote(src, dst, face_send.at[kind, e], face_recv.at[kind, e], device)

    @pl.loop(0, edges)
    def _(e):
        @pl.when(has_down)
        def _():
            face(0, e).start()
            face(1, e).start()

        @pl.when(has_up)
        def _():
            face(2, e).start()
            face(3, e).start()

    for copy in small:
        copy.wait()

    @pl.when(depth == 0)
    def _():
        moist[0] = moist[0] + face_scale * rain[...]

    @pl.loop(0, chunks)
    def _(i):
        chunk = (i + chunks - 1) % chunks
        stage2(chunk).wait_recv()
        here = pl.ds(pl.multiple_of(chunk * R, R), R)
        there = pl.ds(pl.multiple_of(PAD + chunk * R, R), R)
        trans, store, charge = (
            (part[chunk, core, chip, q] + recv1[chunk, chip, q]) + recv2[chunk, q] for q in range(3)
        )
        store = spec_yield + store * layer_thick
        kind = code[here, :]
        river = jnp.where(kind == 1, river_cond, jnp.where(kind == 2, fixed_cond, 0.0))
        old = h0[here, :]
        E[0, there, mid] = trans * layer_thick
        E[1, there, mid] = store + river
        E[2, there, mid] = store * old + charge * (leak_rate * layer_thick) + river * sec[here, :]
        E[3, there, mid] = old

    lane = lax.broadcasted_iota(jnp.int32, (rows_all, LANES), 1) // 8

    def column_halo(side):
        return remote(
            colsend.at[side], colrecv.at[side], col_send.at[side], col_recv.at[side], (below, above)[side]
        )

    def pack(side):
        edge = pl.ds(LANES + (tile - LANES if side == 0 else 0), LANES)
        out = jnp.zeros((rows_all, LANES), jnp.float32)
        for q in range(4):
            shift = (8 * q + (8 if side == 0 else 0)) % LANES
            value = E[q, body, edge]
            out = jnp.where(lane == q, pltpu.roll(value, shift, 1) if shift else value, out)
        colsend[side] = out
        column_halo(side).start()

    def unpack(side):
        column_halo(side).wait_recv()
        value = colrecv[side]
        for q in range(4):
            shift = ((120 if side == 0 else LANES) - 8 * q) % LANES
            E[q, body, pl.ds(0 if side == 0 else LANES + tile, LANES)] = (
                pltpu.roll(value, shift, 1) if shift else value
            )

    def outside(side):
        for q in range(4):
            E[q, body, pl.ds(0 if side == 0 else LANES + tile, LANES)] = jnp.full(
                (rows_all, LANES), 1.0 if q == 1 else 0.0, jnp.float32
            )

    pl.when(has_down)(lambda: pack(0))
    pl.when(has_up)(lambda: pack(1))

    def face_step(e):
        where = pl.ds(pl.multiple_of(e * RE, RE), RE)

        @pl.when(has_down)
        def _():
            face(2, e).wait_recv()
            face(3, e).wait_recv()
            value = flux(pbuf[last, where, part_b], c7[where, part_b], up_p[where], up_c[where])
            fb_out[where] = value
            face(4, e).start()
            moist[last, where, part_b] = moist[last, where, part_b] - value

        @pl.when(has_up)
        def _():
            face(0, e).wait_recv()
            face(1, e).wait_recv()
            value = flux(dn_p[where], dn_c[where], pbuf[0, where, part_a], c0[where, part_a])
            fa_out[where] = value
            face(5, e).start()
            moist[0, where, part_a] = moist[0, where, part_a] + value

    pl.when(has_up)(lambda: unpack(0))
    pl.when(has_down)(lambda: unpack(1))
    pl.when(depth == 0)(lambda: outside(0))
    pl.when(depth == 3)(lambda: outside(1))

    def row_halo(side):
        mine = pl.ds(PAD if side == 0 else PAD + rows_all - 8, 8)
        theirs = pl.ds(PAD + rows_all if side == 0 else PAD - 8, 8)
        return remote(
            E.at[:, mine, :], E.at[:, theirs, :], row_send.at[side], row_recv.at[side], (north, south)[side]
        )

    pl.when(has_north)(lambda: row_halo(0).start())
    pl.when(has_south)(lambda: row_halo(1).start())

    for e in range(edges // 2):
        face_step(e)

    pl.when(has_south)(lambda: row_halo(0).wait_recv())
    pl.when(has_north)(lambda: row_halo(1).wait_recv())

    tiles = rows_all // 8 + 2
    sub = lax.broadcasted_iota(jnp.int32, (8, wide), 0)

    def rows_of(t):
        return pl.ds(pl.multiple_of(8 * t, 8), 8)

    def shift_down(ref, q, t):
        return jnp.where(sub == 0, pltpu.roll(ref[q, rows_of(t - 1), :], 1, 0), pltpu.roll(ref[q, rows_of(t), :], 1, 0))

    def shift_up(ref, q, t):
        return jnp.where(sub == 7, pltpu.roll(ref[q, rows_of(t + 1), :], 7, 0), pltpu.roll(ref[q, rows_of(t), :], 7, 0))

    @pl.loop(1, tiles + 1)
    def _(t):
        here = rows_of(t)
        trans = E[0, here, :]
        east = jnp.sqrt(trans * pltpu.roll(trans, wide - 1, 1))
        west = pltpu.roll(east, 1, 1)
        down = jnp.sqrt(trans * shift_up(E, 0, t))
        up = jnp.sqrt(trans * shift_down(E, 0, t))
        scale = 1.0 / (E[1, here, :] + east + west + down + up)
        C[0, here, :] = E[2, here, :] * scale
        C[1, here, :] = east * scale
        C[2, here, :] = west * scale
        C[3, here, :] = down * scale
        C[4, here, :] = up * scale

    for sweep in range(SWEEPS):
        src, q = (E, 3) if sweep == 0 else (H, (sweep - 1) % 2)

        @pl.loop(1, tiles + 1)
        def _(t):
            here = rows_of(t)
            value = src[q, here, :]
            H[sweep % 2, here, :] = (
                C[0, here, :]
                + C[1, here, :] * pltpu.roll(value, wide - 1, 1)
                + C[2, here, :] * pltpu.roll(value, 1, 1)
                + C[3, here, :] * shift_up(src, q, t)
                + C[4, here, :] * shift_down(src, q, t)
            )

    done = (SWEEPS - 1) % 2
    heads[depth] = H[done, body, mid]
    head[...] = H[done, body, mid]

    def send_head():
        return remote(heads.at[depth], heads.at[depth], head_send.at[0], head_recv.at[depth], {"depth": 3})

    pl.when(depth < 3)(lambda: send_head().start())

    for e in range(edges // 2, edges):
        face_step(e)

    @pl.loop(0, edges)
    def _(e):
        where = pl.ds(pl.multiple_of(e * RE, RE), RE)

        @pl.when(has_down)
        def _():
            face(5, e).wait_recv()
            moist[last, where, part_a] = moist[last, where, part_a] - fa_in[where]

        @pl.when(has_up)
        def _():
            face(4, e).wait_recv()
            moist[0, where, part_b] = moist[0, where, part_b] + fb_in[where]

    @pl.when(depth == 3)
    def _():
        for block in range(4):
            if block < 3:
                remote(heads.at[block], heads.at[block], head_send.at[0], head_recv.at[block], {"depth": 0}).wait_recv()
            cols = pl.ds(block * tile, tile)
            bottom = c7[:, cols] * (
                (pbuf[last, :, cols] - heads[block]) * (2.0 * face_scale / layer_thick) + face_scale
            )
            moist[last, :, cols] = moist[last, :, cols] - bottom

    @pl.loop(0, chunks)
    def _(i):
        stage1(i).wait_send()
        stage2(i).wait_send()

    @pl.loop(0, edges)
    def _(e):
        @pl.when(has_down)
        def _():
            for kind in (0, 1, 4):
                face(kind, e).wait_send()

        @pl.when(has_up)
        def _():
            for kind in (2, 3, 5):
                face(kind, e).wait_send()

    pl.when(has_down)(lambda: column_halo(0).wait_send())
    pl.when(has_up)(lambda: column_halo(1).wait_send())
    pl.when(has_north)(lambda: row_halo(0).wait_send())
    pl.when(has_south)(lambda: row_halo(1).wait_send())
    pl.when(depth < 3)(lambda: send_head().wait_send())


def shards(strips, pressure, texture, active, rain, k_sat, alpha, theta_sat, head_old, cell_code, section):
    layers, rows, cols = pressure.shape
    tile = head_old.shape[1]
    wide = tile + 2 * LANES
    cols_a = tile
    cols_b = cols - cols_a
    chunks, edges = rows // R, rows // RE
    f32 = jnp.float32
    vmem = lambda *shape: pltpu.VMEM(shape, f32)
    dma = lambda *shape: pltpu.SemaphoreType.DMA(shape)
    scratch = [
        vmem(layers, rows, cols),
        pltpu.VMEM((layers, rows, cols), jnp.int32),
        pltpu.VMEM((layers, rows, cols), jnp.int32),
        vmem(rows, cols),
        vmem(rows, tile),
        pltpu.VMEM((rows, tile), jnp.int32),
        vmem(rows, tile),
        vmem(3, 2, 8, LANES),
        vmem(chunks, 2, 2, 3, R, tile),
        vmem(chunks, 2, 3, R, tile),
        vmem(chunks, 3, R, tile),
        vmem(chunks, 3, R, tile),
        vmem(rows, cols),
        vmem(rows, cols),
        vmem(rows, cols_a),
        vmem(rows, cols_a),
        vmem(rows, cols_b),
        vmem(rows, cols_b),
        vmem(rows, cols_b),
        vmem(rows, cols_b),
        vmem(rows, cols_a),
        vmem(rows, cols_a),
        vmem(4, rows + 2 * PAD, wide),
        vmem(2, rows + 2 * PAD, wide),
        vmem(5, rows + 2 * PAD, wide),
        vmem(2, rows, LANES),
        vmem(2, rows, LANES),
        vmem(4, rows, tile),
        dma(3, chunks),
        dma(4),
        dma(chunks),
        dma(chunks),
        dma(chunks),
        dma(chunks),
        dma(6, edges),
        dma(6, edges),
        dma(2),
        dma(2),
        dma(2),
        dma(2),
        dma(1),
        dma(4),
    ]
    anywhere = pl.BlockSpec(memory_space=pltpu.HBM)
    return pl.pallas_call(
        functools.partial(kernel, strips),
        out_shape=(
            pltpu.VMEM((layers, rows, cols), f32),
            pltpu.VMEM((rows, tile), f32),
        ),
        in_specs=[pl.BlockSpec(memory_space=pltpu.SMEM)] * 3 + [anywhere] * 7,
        out_specs=(pl.BlockSpec(memory_space=pltpu.VMEM), pl.BlockSpec(memory_space=pltpu.VMEM)),
        scratch_shapes=scratch,
        compiler_params=pltpu.CompilerParams(
            collective_id=0, has_side_effects=True, vmem_limit_bytes=59 * 2**20
        ),
        name="soil_column",
    )(k_sat, alpha, theta_sat, pressure, texture, active, rain, head_old, cell_code, section)


def solution(mesh):
    in_specs = (
        P("depth", "strips", None),
        P("depth", "strips", None),
        P("depth", "strips", None),
        P("strips", None),
        P(),
        P(),
        P(),
        P("strips", "depth"),
        P("strips", "depth"),
        P("strips", "depth"),
    )
    out_specs = (P("depth", "strips", None), P("strips", "depth"))
    body = functools.partial(shards, mesh.shape["strips"])
    return jax.shard_map(body, mesh=mesh, in_specs=in_specs, out_specs=out_specs, check_vma=False)
```

```python
import functools
import math

import jax
import jax.numpy as jnp
from jax import lax
from jax.experimental import pallas as pl
from jax.experimental.pallas import tpu as pltpu
from jax.sharding import PartitionSpec as P

MESH = pl.DeviceIdType.MESH
SWEEPS = 3

layer_thick = 0.05
soil_step = 0.0002
spec_yield = 0.02
leak_rate = 0.5
river_cond = 0.5
fixed_cond = 3.0
face_scale = soil_step / layer_thick

R = 16
RE = R
LAG = 4
PAD = 16
LANES = 128


def pick(table, index):
    dims = lax.GatherDimensionNumbers(
        offset_dims=(),
        collapsed_slice_dims=(0,),
        start_index_map=(0,),
        operand_batching_dims=(1,),
        start_indices_batching_dims=(1,),
    )
    rows = [
        lax.gather(
            table,
            index[8 * i : 8 * i + 8, :, None],
            dims,
            slice_sizes=(1, 1),
            mode=lax.GatherScatterMode.PROMISE_IN_BOUNDS,
        )
        for i in range(index.shape[0] // 8)
    ]
    return jnp.concatenate(rows, axis=0)


def flux(psi_up, cond_up, psi_low, cond_low):
    return (cond_up + cond_low) * (
        (psi_up - psi_low) * (0.5 * face_scale / layer_thick) + 0.5 * face_scale
    )


def kernel(
    strips, ks_hbm, al_hbm, th_hbm, p_hbm, t_hbm, a_hbm, rain_hbm, h_hbm, code_hbm, sec_hbm,
    moist, head,
    ks, al, th, pbuf, tbuf, abuf, rain, h0, code, sec, tabs, part, recv1, xs, recv2, c0, c7,
    dn_p, dn_c, up_p, up_c, fb_out, fb_in, fa_out, fa_in,
    E, H, C, colsend, colrecv, heads,
    load_sem, misc_sem, s1_send, s1_recv, s2_send, s2_recv,
    face_send, face_recv, col_send, col_recv, row_send, row_recv, head_send, head_recv,
):
    layers, rows_all, cols_all = pbuf.shape
    chunks, edges = rows_all // R, rows_all // RE
    tile = h0.shape[1]
    wide = tile + 2 * LANES
    cols_a = dn_p.shape[1]
    part_a, part_b = pl.ds(0, cols_a), pl.ds(cols_a, cols_all - cols_a)
    body = pl.ds(PAD, rows_all)
    mid = pl.ds(LANES, tile)
    last = layers - 1
    depth, strip = lax.axis_index("depth"), lax.axis_index("strips")
    core, chip = depth % 2, depth // 2
    mate = {"depth": chip * 2 + 1 - core}
    cross = {"depth": (depth + 2) % 4}
    above, below = {"depth": depth - 1}, {"depth": depth + 1}
    north, south = {"strips": strip - 1}, {"strips": strip + 1}
    early = edges // 3
    has_up, has_down = depth > 0, depth < 3
    has_north, has_south = strip > 0, strip < strips - 1

    def remote(src, dst, send, recv, device):
        return pltpu.make_async_remote_copy(
            src_ref=src, dst_ref=dst, send_sem=send, recv_sem=recv,
            device_id=device, device_id_type=MESH,
        )

    barrier = pltpu.get_barrier_semaphore()

    def greet(device):
        pl.semaphore_signal(barrier, inc=1, device_id=device, device_id_type=MESH)

    for step in (1, 2, 3):
        greet({"depth": (depth + step) % 4})
    pl.when(has_north)(lambda: greet(north))
    pl.when(has_south)(lambda: greet(south))

    def load(which, chunk):
        src, dst = ((p_hbm, pbuf), (t_hbm, tbuf), (a_hbm, abuf))[which]
        where = pl.ds(pl.multiple_of(chunk * R, R), R)
        return pltpu.make_async_copy(src.at[:, where, :], dst.at[:, where, :], load_sem.at[which, chunk])

    small = [
        pltpu.make_async_copy(src, dst, misc_sem.at[i])
        for i, (src, dst) in enumerate(((h_hbm, h0), (code_hbm, code), (sec_hbm, sec), (rain_hbm, rain)))
    ]
    tables = [
        pltpu.make_async_copy(src, dst, misc_sem.at[4 + i])
        for i, (src, dst) in enumerate(((ks_hbm, ks), (al_hbm, al), (th_hbm, th)))
    ]
    for copy in tables:
        copy.start()
    for i in range(chunks):
        for which in range(3):
            load(which, (i + chunks - 1) % chunks).start()
    for copy in small:
        copy.start()

    for copy in tables:
        copy.wait()
    scales = (1.0, 0.5 * math.log2(math.e), 0.85)
    row = lax.broadcasted_iota(jnp.int32, (8, LANES), 0)
    for i, (ref, scale) in enumerate(zip((ks, al, th), scales)):
        low = high = jnp.zeros((8, LANES), jnp.float32)
        for c in range(ref.shape[0]):
            value = ref[c] * scale
            if c < 8:
                low = jnp.where(row == c, value, low)
            else:
                high = jnp.where(row == c - 8, value, high)
        tabs[i, 0] = low
        tabs[i, 1] = high

    def blank(first, count):
        for q in range(4):
            E[q, first : first + count, :] = jnp.full((count, wide), 1.0 if q == 1 else 0.0, jnp.float32)

    blank(0, 8)
    blank(PAD + rows_all + 8, 8)
    pl.when(strip == 0)(lambda: blank(8, 8))
    pl.when(strip == strips - 1)(lambda: blank(PAD + rows_all, 8))
    for side in range(SWEEPS):
        H[side, 0:8, :] = jnp.zeros((8, wide), jnp.float32)
        H[side, 2 * PAD + rows_all - 8 :, :] = jnp.zeros((8, wide), jnp.float32)

    def outside(side):
        for q in range(4):
            E[q, body, pl.ds(0 if side == 0 else LANES + tile, LANES)] = jnp.full(
                (rows_all, LANES), 1.0 if q == 1 else 0.0, jnp.float32
            )

    pl.when(depth == 0)(lambda: outside(0))
    pl.when(depth == 3)(lambda: outside(1))

    def order(i):
        return (i + chunks - 1) % chunks

    def stage1(chunk):
        return remote(
            part.at[chunk, 1 - core], recv1.at[chunk], s1_send.at[chunk], s1_recv.at[chunk], mate
        )

    def stage2(chunk):
        return remote(xs.at[chunk], recv2.at[chunk], s2_send.at[chunk], s2_recv.at[chunk], cross)

    def column_pass(chunk):
        for which in range(3):
            load(which, chunk).wait()
        where = pl.ds(pl.multiple_of(chunk * R, R), R)

        def lane_tile(block, half):
            cols = pl.ds(pl.multiple_of(block * tile + half * LANES, LANES), LANES)
            total = None
            for k in range(layers):
                p, t, a = pbuf[k, where, cols], tbuf[k, where, cols], abuf[k, where, cols]
                index, upper = t & 7, t >= 8
                sat, shape, pore = (
                    jnp.where(upper, pick(tabs[i, 1], index), pick(tabs[i, 0], index)) for i in range(3)
                )
                wet = jnp.exp2(shape * jnp.minimum(p, 0.0))
                cond = sat * (wet * wet) * a.astype(jnp.float32)
                dry = pore * (1.0 - wet)
                water = pore * (1.0 / 0.85) - dry
                charge = cond * wet
                if k == 0:
                    c0[where, cols] = cond
                    total = (cond, dry, charge)
                else:
                    total = (total[0] + cond, total[1] + dry, total[2] + charge)
                    inner = flux(p_up, cond_up, p, cond)
                    moist[k - 1, where, cols] = water_up - inner
                    water = water + inner
                p_up, cond_up, water_up = p, cond, water
            moist[last, where, cols] = water_up
            c7[where, cols] = cond_up
            for q in range(3):
                part[chunk, block % 2, block // 2, q, :, half * LANES : (half + 1) * LANES] = total[q]

        @pl.loop(0, cols_all // tile)
        def _(block):
            for half in range(tile // LANES):
                lane_tile(block, half)

    def face(kind, e):
        where = pl.ds(pl.multiple_of(e * RE, RE), RE)
        src, dst, device = (
            (p_hbm.at[last, where, part_a], dn_p.at[where], below),
            (c7.at[where, part_a], dn_c.at[where], below),
            (p_hbm.at[0, where, part_b], up_p.at[where], above),
            (c0.at[where, part_b], up_c.at[where], above),
            (fb_out.at[where], fb_in.at[where], below),
            (fa_out.at[where], fa_in.at[where], above),
        )[kind]
        return remote(src, dst, face_send.at[kind, e], face_recv.at[kind, e], device)

    def finish(chunk):
        stage2(chunk).wait_recv()
        here = pl.ds(pl.multiple_of(chunk * R, R), R)
        there = pl.ds(pl.multiple_of(PAD + chunk * R, R), R)
        trans, store, charge = (
            (part[chunk, core, chip, q] + recv1[chunk, chip, q]) + recv2[chunk, q] for q in range(3)
        )
        store = spec_yield + store * layer_thick
        kind = code[here, :]
        river = jnp.where(kind == 1, river_cond, jnp.where(kind == 2, fixed_cond, 0.0))
        old = h0[here, :]
        E[0, there, mid] = trans * layer_thick
        E[1, there, mid] = store + river
        E[2, there, mid] = store * old + charge * (leak_rate * layer_thick) + river * sec[here, :]
        E[3, there, mid] = old
        pl.when(has_down)(lambda: pack(0, chunk))
        pl.when(has_up)(lambda: pack(1, chunk))

    lane = lax.broadcasted_iota(jnp.int32, (R, LANES), 1) // 8

    def column_halo(side, chunk):
        where = pl.ds(pl.multiple_of(chunk * R, R), R)
        return remote(
            colsend.at[side, where], colrecv.at[side, where],
            col_send.at[side, chunk], col_recv.at[side, chunk], (below, above)[side],
        )

    def pack(side, chunk):
        edge = pl.ds(LANES + (tile - LANES if side == 0 else 0), LANES)
        there = pl.ds(pl.multiple_of(PAD + chunk * R, R), R)
        out = jnp.zeros((R, LANES), jnp.float32)
        for q in range(4):
            shift = (8 * q + (8 if side == 0 else 0)) % LANES
            value = E[q, there, edge]
            out = jnp.where(lane == q, pltpu.roll(value, shift, 1) if shift else value, out)
        colsend[side, pl.ds(pl.multiple_of(chunk * R, R), R)] = out
        column_halo(side, chunk).start()

    def unpack_side(side, chunk):
        there = pl.ds(pl.multiple_of(PAD + chunk * R, R), R)
        column_halo(side, chunk).wait_recv()
        value = colrecv[side, pl.ds(pl.multiple_of(chunk * R, R), R)]
        for q in range(4):
            shift = ((120 if side == 0 else LANES) - 8 * q) % LANES
            E[q, there, pl.ds(0 if side == 0 else LANES + tile, LANES)] = (
                pltpu.roll(value, shift, 1) if shift else value
            )

    def unpack(chunk):
        pl.when(has_up)(lambda: unpack_side(0, chunk))
        pl.when(has_down)(lambda: unpack_side(1, chunk))

    def row_halo(side):
        mine = pl.ds(PAD if side == 0 else PAD + rows_all - 8, 8)
        theirs = pl.ds(PAD + rows_all if side == 0 else PAD - 8, 8)
        return remote(
            E.at[:, mine, :], E.at[:, theirs, :], row_send.at[side], row_recv.at[side], (north, south)[side]
        )

    @pl.loop(0, chunks + 1)
    def _(i):
        @pl.when(i < chunks)
        def _():
            column_pass(order(i))

        @pl.when(i == 0)
        def _():
            pl.semaphore_wait(barrier, 3 + (strip + strips - 1) // strips + (2 * strips - 2 - strip) // strips)

            @pl.loop(0, edges)
            def _(e):
                pl.when(has_down)(lambda: face(0, e).start())

            @pl.loop(0, early)
            def _(e):
                pl.when(has_up)(lambda: face(2, e).start())

            for copy in small:
                copy.wait()

        @pl.when(i > 0)
        def _():
            chunk = order(i - 1)
            stage1(chunk).wait_recv()
            xs[chunk] = part[chunk, core, 1 - chip] + recv1[chunk, 1 - chip]

        @pl.when(i < chunks)
        def _():
            stage1(order(i)).start()

        @pl.when(i > 0)
        def _():
            stage2(order(i - 1)).start()

        @pl.when(i >= LAG)
        def _():
            finish(order(i - LAG))

        @pl.when(i == LAG + 3)
        def _():
            unpack(chunks - 1)
            unpack(0)
            pl.when(has_north)(lambda: row_halo(0).start())
            pl.when(has_south)(lambda: row_halo(1).start())

    @pl.loop(0, edges)
    def _(e):
        @pl.when(has_down)
        def _():
            face(1, e).start()

        @pl.when(has_up)
        def _():
            pl.when(e >= early)(lambda: face(2, e).start())
            face(3, e).start()

    @pl.when(depth == 0)
    def _():
        moist[0] = moist[0] + face_scale * rain[...]

    def face_step(e):
        where = pl.ds(pl.multiple_of(e * RE, RE), RE)

        @pl.when(has_down)
        def _():
            face(2, e).wait_recv()
            face(3, e).wait_recv()
            value = flux(pbuf[last, where, part_b], c7[where, part_b], up_p[where], up_c[where])
            fb_out[where] = value
            moist[last, where, part_b] = moist[last, where, part_b] - value
            face(4, e).start()

        @pl.when(has_up)
        def _():
            face(0, e).wait_recv()
            face(1, e).wait_recv()
            value = flux(dn_p[where], dn_c[where], pbuf[0, where, part_a], c0[where, part_a])
            fa_out[where] = value
            moist[0, where, part_a] = moist[0, where, part_a] + value
            face(5, e).start()

    sub = lax.broadcasted_iota(jnp.int32, (8, wide), 0)

    def rows_of(t):
        return pl.ds(pl.multiple_of(8 * t, 8), 8)

    def shift_down(ref, q, t):
        return jnp.where(sub == 0, pltpu.roll(ref[q, rows_of(t - 1), :], 1, 0), pltpu.roll(ref[q, rows_of(t), :], 1, 0))

    def shift_up(ref, q, t):
        return jnp.where(sub == 7, pltpu.roll(ref[q, rows_of(t + 1), :], 7, 0), pltpu.roll(ref[q, rows_of(t), :], 7, 0))

    def coefficients(t):
        here = rows_of(t)
        trans = E[0, here, :]
        east = jnp.sqrt(trans * pltpu.roll(trans, wide - 1, 1))
        west = pltpu.roll(east, 1, 1)
        down = jnp.sqrt(trans * shift_up(E, 0, t))
        up = jnp.sqrt(trans * shift_down(E, 0, t))
        scale = 1.0 / (E[1, here, :] + east + west + down + up)
        C[0, here, :] = E[2, here, :] * scale
        C[1, here, :] = east * scale
        C[2, here, :] = west * scale
        C[3, here, :] = down * scale
        C[4, here, :] = up * scale

    def sweep(n, t):
        src, q = (E, 3) if n == 0 else (H, n - 1)
        here = rows_of(t)
        value = src[q, here, :]
        H[n, here, :] = (
            C[0, here, :]
            + C[1, here, :] * pltpu.roll(value, wide - 1, 1)
            + C[2, here, :] * pltpu.roll(value, 1, 1)
            + C[3, here, :] * shift_up(src, q, t)
            + C[4, here, :] * shift_down(src, q, t)
        )

    tiles = rows_all // 8 + 2

    def wave(t, first=0, final=False):
        if not final:
            coefficients(t)
            sweep(0, t)
        for n in range(1, SWEEPS):
            if first == 0 or t - n >= n:
                sweep(n, t - n)

    def head_copy(chunk, source):
        where = pl.ds(pl.multiple_of(chunk * R, R), R)
        return remote(
            heads.at[source, where], heads.at[source, where],
            head_send.at[chunk], head_recv.at[source, chunk], {"depth": 3},
        )

    def hand_on(chunk):
        where = pl.ds(pl.multiple_of(chunk * R, R), R)
        value = H[SWEEPS - 1, pl.ds(pl.multiple_of(PAD + chunk * R, R), R), mid]
        heads[depth, where] = value
        head[where, :] = value
        pl.when(depth < 3)(lambda: head_copy(chunk, depth).start())

    for i in range(chunks + 1 - LAG, chunks):
        finish((i + chunks - 1) % chunks)
    for i in range(2, 5):
        unpack((i + chunks - 1) % chunks)

    pl.when(has_south)(lambda: row_halo(0).wait_recv())
    pl.when(has_north)(lambda: row_halo(1).wait_recv())

    for t in (1, 2, 3):
        wave(t, first=1)
    wave(4)

    @pl.loop(2, 4)
    def _(chunk):
        wave(2 * chunk + 1)
        wave(2 * chunk + 2)
        hand_on(chunk - 2)

    face_step(0)
    face_step(1)

    @pl.loop(4, chunks - 1)
    def _(chunk):
        unpack(chunk)
        wave(2 * chunk + 1)
        wave(2 * chunk + 2)
        hand_on(chunk - 2)
        face_step(chunk - 2)

    for t in range(tiles - 3, tiles + 1):
        wave(t)
    hand_on(chunks - 3)
    hand_on(chunks - 2)
    wave(tiles + 1, final=True)
    hand_on(chunks - 1)

    @pl.loop(chunks - 3, edges)
    def _(e):
        face_step(e)

    @pl.loop(0, edges)
    def _(e):
        where = pl.ds(pl.multiple_of(e * RE, RE), RE)

        @pl.when(depth == 3)
        def _():
            for block in range(4):
                if block < 3:
                    head_copy(e, block).wait_recv()
                cols = pl.ds(block * tile, tile)
                bottom = c7[where, cols] * (
                    (pbuf[last, where, cols] - heads[block, where]) * (2.0 * face_scale / layer_thick) + face_scale
                )
                moist[last, where, cols] = moist[last, where, cols] - bottom

        @pl.when(has_down)
        def _():
            face(5, e).wait_recv()
            moist[last, where, part_a] = moist[last, where, part_a] - fa_in[where]

        @pl.when(has_up)
        def _():
            face(4, e).wait_recv()
            moist[0, where, part_b] = moist[0, where, part_b] + fb_in[where]

    @pl.loop(0, chunks)
    def _(i):
        stage1(i).wait_send()
        stage2(i).wait_send()

        @pl.when(has_down)
        def _():
            for kind in (0, 1, 4):
                face(kind, i).wait_send()
            column_halo(0, i).wait_send()
            head_copy(i, depth).wait_send()

        @pl.when(has_up)
        def _():
            for kind in (2, 3, 5):
                face(kind, i).wait_send()
            column_halo(1, i).wait_send()

    pl.when(has_north)(lambda: row_halo(0).wait_send())
    pl.when(has_south)(lambda: row_halo(1).wait_send())


def store_kernel(moist, head, moist_out, head_out, sems):
    copies = [pltpu.make_async_copy(head, head_out, sems.at[0])]
    for k in range(moist.shape[0]):
        copies.append(pltpu.make_async_copy(moist.at[k], moist_out.at[k], sems.at[k + 1]))
    for copy in copies:
        copy.start()
    for copy in copies:
        copy.wait()


def shards(strips, pressure, texture, active, rain, k_sat, alpha, theta_sat, head_old, cell_code, section):
    layers, rows, cols = pressure.shape
    tile = head_old.shape[1]
    wide = tile + 2 * LANES
    cols_a = tile
    cols_b = cols - cols_a
    chunks, edges = rows // R, rows // RE
    f32 = jnp.float32
    vmem = lambda *shape: pltpu.VMEM(shape, f32)
    dma = lambda *shape: pltpu.SemaphoreType.DMA(shape)
    table = pltpu.SMEM(k_sat.shape, f32)
    scratch = [
        table,
        table,
        table,
        vmem(layers, rows, cols),
        pltpu.VMEM((layers, rows, cols), jnp.int32),
        pltpu.VMEM((layers, rows, cols), jnp.int32),
        vmem(rows, cols),
        vmem(rows, tile),
        pltpu.VMEM((rows, tile), jnp.int32),
        vmem(rows, tile),
        vmem(3, 2, 8, LANES),
        vmem(chunks, 2, 2, 3, R, tile),
        vmem(chunks, 2, 3, R, tile),
        vmem(chunks, 3, R, tile),
        vmem(chunks, 3, R, tile),
        vmem(rows, cols),
        vmem(rows, cols),
        vmem(rows, cols_a),
        vmem(rows, cols_a),
        vmem(rows, cols_b),
        vmem(rows, cols_b),
        vmem(rows, cols_b),
        vmem(rows, cols_b),
        vmem(rows, cols_a),
        vmem(rows, cols_a),
        vmem(4, rows + 2 * PAD, wide),
        vmem(SWEEPS, rows + 2 * PAD, wide),
        vmem(5, rows + 2 * PAD, wide),
        vmem(2, rows, LANES),
        vmem(2, rows, LANES),
        vmem(4, rows, tile),
        dma(3, chunks),
        dma(7),
        dma(chunks),
        dma(chunks),
        dma(chunks),
        dma(chunks),
        dma(6, edges),
        dma(6, edges),
        dma(2, chunks),
        dma(2, chunks),
        dma(2),
        dma(2),
        dma(chunks),
        dma(4, chunks),
    ]
    anywhere = pl.BlockSpec(memory_space=pltpu.HBM)
    moist, head = pl.pallas_call(
        functools.partial(kernel, strips),
        out_shape=(
            pltpu.VMEM((layers, rows, cols), f32),
            pltpu.VMEM((rows, tile), f32),
        ),
        in_specs=[anywhere] * 10,
        out_specs=(pl.BlockSpec(memory_space=pltpu.VMEM), pl.BlockSpec(memory_space=pltpu.VMEM)),
        scratch_shapes=scratch,
        compiler_params=pltpu.CompilerParams(
            collective_id=0, has_side_effects=True, vmem_limit_bytes=59 * 2**20
        ),
        name="soil_column",
    )(k_sat, alpha, theta_sat, pressure, texture, active, rain, head_old, cell_code, section)
    on_chip = pl.BlockSpec(memory_space=pltpu.VMEM)
    return pl.pallas_call(
        store_kernel,
        out_shape=(
            jax.ShapeDtypeStruct((layers, rows, cols), f32),
            jax.ShapeDtypeStruct((rows, tile), f32),
        ),
        in_specs=[on_chip] * 2,
        out_specs=(anywhere, anywhere),
        scratch_shapes=[dma(layers + 1)],
        compiler_params=pltpu.CompilerParams(vmem_limit_bytes=2**20),
        name="store",
    )(pltpu.with_memory_space_constraint(moist, pltpu.VMEM), pltpu.with_memory_space_constraint(head, pltpu.VMEM))


def solution(mesh):
    in_specs = (
        P("depth", "strips", None),
        P("depth", "strips", None),
        P("depth", "strips", None),
        P("strips", None),
        P(),
        P(),
        P(),
        P("strips", "depth"),
        P("strips", "depth"),
        P("strips", "depth"),
    )
    out_specs = (P("depth", "strips", None), P("strips", "depth"))
    body = functools.partial(shards, mesh.shape["strips"])
    return jax.shard_map(body, mesh=mesh, in_specs=in_specs, out_specs=out_specs, check_vma=False)
```

```python
import functools
import math

import jax
import jax.numpy as jnp
from jax import lax
from jax.experimental import pallas as pl
from jax.experimental.pallas import tpu as pltpu
from jax.sharding import PartitionSpec as P

MESH = pl.DeviceIdType.MESH
SWEEPS = 3

layer_thick = 0.05
soil_step = 0.0002
spec_yield = 0.02
leak_rate = 0.5
river_cond = 0.5
fixed_cond = 3.0
face_scale = soil_step / layer_thick

R = 16
RE = R
PAD = 24
LANES = 128


def pick(table, index):
    dims = lax.GatherDimensionNumbers(
        offset_dims=(),
        collapsed_slice_dims=(0,),
        start_index_map=(0,),
        operand_batching_dims=(1,),
        start_indices_batching_dims=(1,),
    )
    rows = [
        lax.gather(
            table,
            index[8 * i : 8 * i + 8, :, None],
            dims,
            slice_sizes=(1, 1),
            mode=lax.GatherScatterMode.PROMISE_IN_BOUNDS,
        )
        for i in range(index.shape[0] // 8)
    ]
    return jnp.concatenate(rows, axis=0)


def flux(psi_up, cond_up, psi_low, cond_low):
    return (cond_up + cond_low) * (
        (psi_up - psi_low) * (0.5 * face_scale / layer_thick) + 0.5 * face_scale
    )


def kernel(
    strips, ks_hbm, al_hbm, th_hbm, p_hbm, t_hbm, a_hbm, rain_hbm, h_hbm, code_hbm, sec_hbm,
    moist, head,
    ks, al, th, pbuf, tbuf, abuf, rain, h0, code, sec, tabs, part, recv1, xs, recv2, c0, c7,
    dn_p, dn_c, up_pc, fb_out, fb_in, fa_out, fa_in,
    E, H, A, colsend, colrecv, heads,
    load_sem, misc_sem, s1_send, s1_recv, s2_send, s2_recv,
    face_send, down_recv, up_recv, fb_recv, fa_recv, col_send, col_recv, row_send, row_recv, head_send, head_recv,
):
    layers, rows_all, cols_all = pbuf.shape
    chunks, edges = rows_all // R, rows_all // RE
    tile = h0.shape[1]
    wide = tile + LANES
    cols_a = dn_p.shape[1]
    part_a, part_b = pl.ds(0, cols_a), pl.ds(cols_a, cols_all - cols_a)
    body = pl.ds(PAD, rows_all)
    mid, halo = pl.ds(0, tile), pl.ds(tile, LANES)
    last = layers - 1
    depth, strip = lax.axis_index("depth"), lax.axis_index("strips")
    core, chip = depth % 2, depth // 2
    mate = {"depth": chip * 2 + 1 - core}
    cross = {"depth": (depth + 2) % 4}
    above, below = {"depth": depth - 1}, {"depth": depth + 1}
    north, south = {"strips": strip - 1}, {"strips": strip + 1}
    early = edges // 3
    has_up, has_down = depth > 0, depth < 3
    has_north, has_south = strip > 0, strip < strips - 1

    def remote(src, dst, send, recv, device):
        return pltpu.make_async_remote_copy(
            src_ref=src, dst_ref=dst, send_sem=send, recv_sem=recv,
            device_id=device, device_id_type=MESH,
        )

    barrier = pltpu.get_barrier_semaphore()

    def greet(device):
        pl.semaphore_signal(barrier, inc=1, device_id=device, device_id_type=MESH)

    for step in (1, 2, 3):
        greet({"depth": (depth + step) % 4})
    pl.when(has_north)(lambda: greet(north))
    pl.when(has_south)(lambda: greet(south))

    def load(which, chunk):
        src, dst = ((p_hbm, pbuf), (t_hbm, tbuf), (a_hbm, abuf))[which]
        where = pl.ds(pl.multiple_of(chunk * R, R), R)
        return pltpu.make_async_copy(src.at[:, where, :], dst.at[:, where, :], load_sem.at[which, chunk])

    small = [
        pltpu.make_async_copy(src, dst, misc_sem.at[i])
        for i, (src, dst) in enumerate(((h_hbm, h0), (code_hbm, code), (sec_hbm, sec), (rain_hbm, rain)))
    ]
    tables = [
        pltpu.make_async_copy(src, dst, misc_sem.at[4 + i])
        for i, (src, dst) in enumerate(((ks_hbm, ks), (al_hbm, al), (th_hbm, th)))
    ]
    for copy in tables:
        copy.start()
    for i in range(chunks):
        for which in range(3):
            load(which, (i + chunks - 1) % chunks).start()
    for copy in small:
        copy.start()

    for copy in tables:
        copy.wait()
    scales = (1.0, 0.5 * math.log2(math.e), 0.85)
    row = lax.broadcasted_iota(jnp.int32, (8, LANES), 0)
    for i, (ref, scale) in enumerate(zip((ks, al, th), scales)):
        low = high = jnp.zeros((8, LANES), jnp.float32)
        for c in range(ref.shape[0]):
            value = ref[c] * scale
            if c < 8:
                low = jnp.where(row == c, value, low)
            else:
                high = jnp.where(row == c - 8, value, high)
        tabs[i, 0] = low
        tabs[i, 1] = high

    def blank(first, count):
        for q in range(4):
            E[q, first : first + count, :] = jnp.full((count, wide), 1.0 if q == 1 else 0.0, jnp.float32)

    blank(0, PAD - 8)
    blank(PAD + rows_all + 8, PAD - 8)
    pl.when(strip == 0)(lambda: blank(PAD - 8, 8))
    pl.when(strip == strips - 1)(lambda: blank(PAD + rows_all, 8))
    for ref in (A, H):
        for q in range(ref.shape[0]):
            ref[q, 0:PAD, :] = jnp.zeros((PAD, wide), jnp.float32)
            ref[q, PAD + rows_all :, :] = jnp.zeros((PAD, wide), jnp.float32)

    def outside(side):
        group = lax.broadcasted_iota(jnp.int32, (8, LANES), 1) // 8
        for chunk in range(chunks + 1):
            colrecv[side, chunk] = jnp.where(group % 4 == 1, 1.0, 0.0)

    pl.when(depth == 0)(lambda: outside(0))
    pl.when(depth == 3)(lambda: outside(1))

    def order(i):
        return (i + chunks - 1) % chunks

    def stage1(chunk):
        return remote(
            part.at[chunk, 1 - core], recv1.at[chunk], s1_send.at[0], s1_recv.at[chunk], mate
        )

    def stage2(chunk):
        return remote(xs.at[chunk], recv2.at[chunk], s2_send.at[0], s2_recv.at[chunk], cross)

    def column_pass(chunk):
        for which in range(3):
            load(which, chunk).wait()
        where = pl.ds(pl.multiple_of(chunk * R, R), R)

        def lane_tile(block, half):
            cols = pl.ds(pl.multiple_of(block * tile + half * LANES, LANES), LANES)
            total = None
            for k in range(layers):
                p, t, a = pbuf[k, where, cols], tbuf[k, where, cols], abuf[k, where, cols]
                index, upper = t & 7, t >= 8
                sat, shape, pore = (
                    jnp.where(upper, pick(tabs[i, 1], index), pick(tabs[i, 0], index)) for i in range(3)
                )
                wet = jnp.exp2(shape * jnp.minimum(p, 0.0))
                cond = sat * (wet * wet) * a.astype(jnp.float32)
                dry = pore * (1.0 - wet)
                water = pore * (1.0 / 0.85) - dry
                charge = cond * wet
                if k == 0:
                    c0[where, cols] = cond
                    total = (cond, dry, charge)
                else:
                    total = (total[0] + cond, total[1] + dry, total[2] + charge)
                    inner = flux(p_up, cond_up, p, cond)
                    moist[k - 1, where, cols] = water_up - inner
                    water = water + inner
                p_up, cond_up, water_up = p, cond, water
            moist[last, where, cols] = water_up
            c7[where, cols] = cond_up
            for q in range(3):
                part[chunk, block % 2, block // 2, q, :, half * LANES : (half + 1) * LANES] = total[q]

        @pl.loop(0, cols_all // tile)
        def _(block):
            for half in range(tile // LANES):
                lane_tile(block, half)

    half = rows_all // 2

    def down_p():
        return remote(p_hbm.at[last, :, part_a], dn_p, face_send.at[0], down_recv.at[0], below)

    def down_c(k):
        where = pl.ds(k * half, half)
        return remote(c7.at[where, part_a], dn_c.at[where], face_send.at[1], down_recv.at[1 + k], below)

    def up_message(which, e):
        where = pl.ds(pl.multiple_of(e * RE, RE), RE)
        src = p_hbm.at[0, where, part_b] if which == 0 else c0.at[where, part_b]
        return remote(src, up_pc.at[e, which], face_send.at[2 + which], up_recv.at[e], above)

    def flux_down(e):
        where = pl.ds(pl.multiple_of(e * RE, RE), RE)
        return remote(fb_out.at[where], fb_in.at[where], face_send.at[4], fb_recv.at[e], below)

    def flux_up(e):
        where = pl.ds(pl.multiple_of(e * RE, RE), RE)
        return remote(fa_out.at[where], fa_in.at[where], face_send.at[5], fa_recv.at[0], above)

    def finish(chunk):
        stage2(chunk).wait_recv()
        here = pl.ds(pl.multiple_of(chunk * R, R), R)
        there = pl.ds(pl.multiple_of(PAD + chunk * R, 8), R)
        trans, store, charge = (
            (part[chunk, core, chip, q] + recv1[chunk, chip, q]) + recv2[chunk, q] for q in range(3)
        )
        store = spec_yield + store * layer_thick
        kind = code[here, :]
        river = jnp.where(kind == 1, river_cond, jnp.where(kind == 2, fixed_cond, 0.0))
        old = h0[here, :]
        root = jnp.sqrt(trans * layer_thick)
        E[0, there, mid] = root
        E[1, there, mid] = store + river
        E[2, there, mid] = store * old + charge * (leak_rate * layer_thick) + river * sec[here, :]
        E[3, there, mid] = root * old
        pack(chunk, tiles_of(chunk))

    lane = lax.broadcasted_iota(jnp.int32, (8, LANES), 1) // 8

    def column_halo(side, chunk):
        return remote(
            colsend.at[side, chunk], colrecv.at[side, chunk],
            col_send.at[side], col_recv.at[side, chunk], (below, above)[side],
        )

    def pack_tiles(side, chunk, tiles):
        edge = pl.ds(tile - LANES if side == 0 else 0, LANES)
        out = jnp.zeros((8, LANES), jnp.float32)
        for q in range(4):
            for h in range(2):
                group = q + 4 * h
                shift = (8 * group + (8 if side == 0 else 0)) % LANES
                value = E[q, tiles[h], edge]
                out = jnp.where(lane == group, pltpu.roll(value, shift, 1) if shift else value, out)
        colsend[side, chunk] = out
        column_halo(side, chunk).start()

    def tiles_of(chunk):
        return [pl.ds(pl.multiple_of(PAD + chunk * R + 8 * h, 8), 8) for h in range(2)]

    halo_tiles = [pl.ds(PAD - 8, 8), pl.ds(PAD + rows_all, 8)]

    def pack(chunk, tiles):
        pl.when(has_down)(lambda: pack_tiles(0, chunk, tiles))
        pl.when(has_up)(lambda: pack_tiles(1, chunk, tiles))

    def unpack(chunk, tiles=None):
        pl.when(has_up)(lambda: column_halo(0, chunk).wait_recv())
        pl.when(has_down)(lambda: column_halo(1, chunk).wait_recv())
        west, east = colrecv[0, chunk], colrecv[1, chunk]
        for q in range(4):
            for h in range(2):
                group = q + 4 * h
                moved = pltpu.roll(west, 120 - 8 * group, 1)
                E[q, (tiles or tiles_of(chunk))[h], halo] = jnp.where(
                    lane < 8, pltpu.roll(east, LANES - 8 * group, 1) if group else east, moved
                )

    def row_halo(side):
        mine = pl.ds(PAD if side == 0 else PAD + rows_all - 8, 8)
        theirs = pl.ds(PAD + rows_all if side == 0 else PAD - 8, 8)
        return remote(
            E.at[:, mine, mid], E.at[:, theirs, mid], row_send.at[side], row_recv.at[side], (north, south)[side]
        )

    @pl.loop(0, chunks + 2)
    def _(i):
        @pl.when(i < chunks)
        def _():
            column_pass(order(i))

        @pl.when(i == 0)
        def _():
            pl.semaphore_wait(barrier, 3 + (strip + strips - 1) // strips + (2 * strips - 2 - strip) // strips)

            pl.when(has_down)(lambda: down_p().start())

            @pl.loop(0, early)
            def _(e):
                pl.when(has_up)(lambda: up_message(0, e).start())

        @pl.when(i == chunks)
        def _():
            for copy in small:
                copy.wait()

        @pl.when(i >= chunks)
        def _():
            finish(order(i - chunks))

        @pl.when(i > 1)
        def _():
            chunk = order(i - 2)
            stage1(chunk).wait_recv()
            xs[chunk] = part[chunk, core, 1 - chip] + recv1[chunk, 1 - chip]

        @pl.when(i < chunks)
        def _():
            stage1(order(i)).start()

        @pl.when(i > 1)
        def _():
            stage2(order(i - 2)).start()

    def post_faces(first, last_one):
        @pl.loop(first, last_one)
        def _(e):
            @pl.when(has_up)
            def _():
                pl.when(e >= early)(lambda: up_message(0, e).start())
                up_message(1, e).start()

    @pl.when(depth == 0)
    def _():
        moist[0] = moist[0] + face_scale * rain[...]

    def face_step(e):
        where = pl.ds(pl.multiple_of(e * RE, RE), RE)

        @pl.when(has_down)
        def _():
            remote(up_pc.at[e], up_pc.at[e], face_send.at[2], up_recv.at[e], below).wait_recv()
            value = flux(pbuf[last, where, part_b], c7[where, part_b], up_pc[e, 0], up_pc[e, 1])
            fb_out[where] = value
            moist[last, where, part_b] = moist[last, where, part_b] - value
            flux_down(e).start()

        @pl.when(has_up)
        def _():
            @pl.when(e == 0)
            def _():
                down_p().wait_recv()
                down_c(0).wait_recv()

            pl.when(e == edges // 2)(lambda: down_c(1).wait_recv())
            value = flux(dn_p[where], dn_c[where], pbuf[0, where, part_a], c0[where, part_a])
            fa_out[where] = value
            moist[0, where, part_a] = moist[0, where, part_a] + value
            flux_up(e).start()

    sub = lax.broadcasted_iota(jnp.int32, (8, wide), 0)

    def rows_of(t, count=1):
        return pl.ds(pl.multiple_of(8 * t, 8), 8 * count)

    def around(ref, q, t):
        north_t, a, b, south_t = (ref[q, rows_of(t + k), :] for k in (-1, 0, 1, 2))

        def sums(before, here, after):
            down = [pltpu.roll(v, 1, 0) for v in (before, here)]
            up = [pltpu.roll(v, 7, 0) for v in (here, after)]
            return (
                pltpu.roll(here, 1, 1)
                + pltpu.roll(here, wide - 1, 1)
                + jnp.where(sub == 0, down[0], down[1])
                + jnp.where(sub == 7, up[1], up[0])
            )

        return jnp.concatenate([sums(north_t, a, b), sums(a, b, south_t)], axis=0)

    def wave(j, stages):
        at = (2 * j + 2, 2 * j, 2 * j - 3, 2 * j - 6)
        out = []
        if 3 in stages:
            here = rows_of(at[3], 2)
            out.append((H, 2, here, A[2, here, :] + A[3, here, :] * around(H, 1, at[3])))
        if 2 in stages:
            here = rows_of(at[2], 2)
            out.append((H, 1, here, A[0, here, :] + A[1, here, :] * around(H, 0, at[2])))
        if 1 in stages:
            here = rows_of(at[1], 2)
            out.append((H, 0, here, A[0, here, :] + A[1, here, :] * around(E, 3, at[1])))
        if 0 in stages:
            here = rows_of(at[0], 2)
            root = E[0, here, :]
            scale = 1.0 / (E[1, here, :] + root * around(E, 0, at[0]))
            free, bound = E[2, here, :] * scale, root * scale
            out += [(A, 0, here, root * free), (A, 1, here, root * bound), (A, 2, here, free), (A, 3, here, bound)]
        for ref, q, here, value in out:
            ref[q, here, :] = value

    def head_copy(chunk, source):
        where = pl.ds(pl.multiple_of(chunk * R, R), R)
        return remote(
            heads.at[source, where], heads.at[source, where],
            head_send.at[0], head_recv.at[source], {"depth": 3},
        )

    def hand_on(chunk):
        where = pl.ds(pl.multiple_of(chunk * R, R), R)
        value = H[SWEEPS - 1, pl.ds(pl.multiple_of(PAD + chunk * R, 8), R), mid]
        heads[depth, where] = value
        head[where, :] = value
        pl.when(depth < 3)(lambda: head_copy(chunk, depth).start())

    pl.when(has_north)(lambda: row_halo(0).start())
    pl.when(has_south)(lambda: row_halo(1).start())

    @pl.loop(1, chunks - 3)
    def _(chunk):
        finish(chunk)

    pl.when(has_down)(lambda: down_c(0).start())
    post_faces(0, 1)
    finish(chunks - 3)
    post_faces(1, 2)
    finish(chunks - 2)
    pl.when(has_down)(lambda: down_c(1).start())

    pl.when(has_south)(lambda: row_halo(0).wait_recv())
    pl.when(has_north)(lambda: row_halo(1).wait_recv())
    pack(chunks, halo_tiles)
    post_faces(2, edges)

    @pl.loop(0, chunks - 3)
    def _(chunk):
        unpack(chunk)

    unpack(chunks - 1)
    unpack(chunks, halo_tiles)

    every = (0, 1, 2, 3)
    wave(0, (0,))
    wave(1, (0, 1))
    wave(2, (0, 1, 2))
    wave(3, (0, 1, 2))
    wave(4, (0, 1, 2, 3))
    face_step(0)

    @pl.loop(5, chunks - 1)
    def _(j):
        unpack(j)
        wave(j, every)
        hand_on(j - 5)

    face_step(1)

    @pl.loop(chunks - 1, chunks + 1)
    def _(j):
        wave(j, every)
        hand_on(j - 5)

    for j, stages in ((chunks + 1, (1, 2, 3)), (chunks + 2, (2, 3)), (chunks + 3, (2, 3)), (chunks + 4, (3,))):
        wave(j, stages)
        hand_on(j - 5)

    @pl.loop(2, edges)
    def _(e):
        face_step(e)

    @pl.when(depth == 3)
    def _():
        for block in range(4):
            if block < 3:
                remote(heads.at[block], heads.at[block], head_send.at[0], head_recv.at[block], {"depth": 0}).wait_recv()
            cols = pl.ds(block * tile, tile)
            bottom = c7[:, cols] * (
                (pbuf[last, :, cols] - heads[block]) * (2.0 * face_scale / layer_thick) + face_scale
            )
            moist[last, :, cols] = moist[last, :, cols] - bottom

    @pl.when(has_down)
    def _():
        remote(fa_in, fa_in, face_send.at[5], fa_recv.at[0], below).wait_recv()
        moist[last, :, part_a] = moist[last, :, part_a] - fa_in[...]

    @pl.when(has_up)
    def _():
        @pl.loop(0, edges)
        def _(e):
            where = pl.ds(pl.multiple_of(e * RE, RE), RE)
            flux_down(e).wait_recv()
            moist[0, where, part_b] = moist[0, where, part_b] + fb_in[where]

    remote(part.at[:, 1 - core], recv1, s1_send.at[0], s1_recv.at[0], mate).wait_send()
    remote(xs, recv2, s2_send.at[0], s2_recv.at[0], cross).wait_send()

    @pl.when(has_down)
    def _():
        down_p().wait_send()
        remote(c7.at[:, part_a], dn_c, face_send.at[1], down_recv.at[1], below).wait_send()
        remote(fb_out, fb_in, face_send.at[4], fb_recv.at[0], below).wait_send()
        remote(colsend.at[0], colrecv.at[0], col_send.at[0], col_recv.at[0, 0], below).wait_send()
        remote(heads.at[depth], heads.at[depth], head_send.at[0], head_recv.at[depth], {"depth": 3}).wait_send()

    @pl.when(has_up)
    def _():
        remote(p_hbm.at[0, :, part_b], fb_in, face_send.at[2], up_recv.at[0], above).wait_send()
        remote(c0.at[:, part_b], fb_in, face_send.at[3], up_recv.at[0], above).wait_send()
        remote(fa_out, fa_in, face_send.at[5], fa_recv.at[0], above).wait_send()
        remote(colsend.at[1], colrecv.at[1], col_send.at[1], col_recv.at[1, 0], above).wait_send()

    pl.when(has_north)(lambda: row_halo(0).wait_send())
    pl.when(has_south)(lambda: row_halo(1).wait_send())


def store_kernel(moist, head, moist_out, head_out, sems):
    copies = [pltpu.make_async_copy(head, head_out, sems.at[0])]
    for k in range(moist.shape[0]):
        copies.append(pltpu.make_async_copy(moist.at[k], moist_out.at[k], sems.at[k + 1]))
    for copy in copies:
        copy.start()
    for copy in copies:
        copy.wait()


def shards(strips, pressure, texture, active, rain, k_sat, alpha, theta_sat, head_old, cell_code, section):
    layers, rows, cols = pressure.shape
    tile = head_old.shape[1]
    wide = tile + LANES
    cols_a = 3 * LANES
    cols_b = cols - cols_a
    chunks, edges = rows // R, rows // RE
    f32 = jnp.float32
    vmem = lambda *shape: pltpu.VMEM(shape, f32)
    dma = lambda *shape: pltpu.SemaphoreType.DMA(shape)
    table = pltpu.SMEM(k_sat.shape, f32)
    scratch = [
        table,
        table,
        table,
        vmem(layers, rows, cols),
        pltpu.VMEM((layers, rows, cols), jnp.int32),
        pltpu.VMEM((layers, rows, cols), jnp.int32),
        vmem(rows, cols),
        vmem(rows, tile),
        pltpu.VMEM((rows, tile), jnp.int32),
        vmem(rows, tile),
        vmem(3, 2, 8, LANES),
        vmem(chunks, 2, 2, 3, R, tile),
        vmem(chunks, 2, 3, R, tile),
        vmem(chunks, 3, R, tile),
        vmem(chunks, 3, R, tile),
        vmem(rows, cols),
        vmem(rows, cols),
        vmem(rows, cols_a),
        vmem(rows, cols_a),
        vmem(edges, 2, RE, cols_b),
        vmem(rows, cols_b),
        vmem(rows, cols_b),
        vmem(rows, cols_a),
        vmem(rows, cols_a),
        vmem(4, rows + 2 * PAD, wide),
        vmem(SWEEPS, rows + 2 * PAD, wide),
        vmem(4, rows + 2 * PAD, wide),
        vmem(2, chunks + 1, 8, LANES),
        vmem(2, chunks + 1, 8, LANES),
        vmem(4, rows, tile),
        dma(3, chunks),
        dma(7),
        dma(1),
        dma(chunks),
        dma(1),
        dma(chunks),
        dma(6),
        dma(3),
        dma(edges),
        dma(edges),
        dma(1),
        dma(2),
        dma(2, chunks + 1),
        dma(2),
        dma(2),
        dma(1),
        dma(4),
    ]
    anywhere = pl.BlockSpec(memory_space=pltpu.HBM)
    moist, head = pl.pallas_call(
        functools.partial(kernel, strips),
        out_shape=(
            pltpu.VMEM((layers, rows, cols), f32),
            pltpu.VMEM((rows, tile), f32),
        ),
        in_specs=[anywhere] * 10,
        out_specs=(pl.BlockSpec(memory_space=pltpu.VMEM), pl.BlockSpec(memory_space=pltpu.VMEM)),
        scratch_shapes=scratch,
        compiler_params=pltpu.CompilerParams(
            collective_id=0, has_side_effects=True, vmem_limit_bytes=59 * 2**20
        ),
        name="soil_column",
    )(k_sat, alpha, theta_sat, pressure, texture, active, rain, head_old, cell_code, section)
    on_chip = pl.BlockSpec(memory_space=pltpu.VMEM)
    return pl.pallas_call(
        store_kernel,
        out_shape=(
            jax.ShapeDtypeStruct((layers, rows, cols), f32),
            jax.ShapeDtypeStruct((rows, tile), f32),
        ),
        in_specs=[on_chip] * 2,
        out_specs=(anywhere, anywhere),
        scratch_shapes=[dma(layers + 1)],
        compiler_params=pltpu.CompilerParams(vmem_limit_bytes=2**20),
        name="store",
    )(pltpu.with_memory_space_constraint(moist, pltpu.VMEM), pltpu.with_memory_space_constraint(head, pltpu.VMEM))


def solution(mesh):
    in_specs = (
        P("depth", "strips", None),
        P("depth", "strips", None),
        P("depth", "strips", None),
        P("strips", None),
        P(),
        P(),
        P(),
        P("strips", "depth"),
        P("strips", "depth"),
        P("strips", "depth"),
    )
    out_specs = (P("depth", "strips", None), P("strips", "depth"))
    body = functools.partial(shards, mesh.shape["strips"])
    return jax.shard_map(body, mesh=mesh, in_specs=in_specs, out_specs=out_specs, check_vma=False)
```

```python
import functools
import math

import jax
import jax.numpy as jnp
from jax import lax
from jax.experimental import pallas as pl
from jax.experimental.pallas import tpu as pltpu
from jax.sharding import PartitionSpec as P

MESH = pl.DeviceIdType.MESH
SWEEPS = 3

layer_thick = 0.05
soil_step = 0.0002
spec_yield = 0.02
leak_rate = 0.5
river_cond = 0.5
fixed_cond = 3.0
face_scale = soil_step / layer_thick

R = 16
RE = R
XS, YS = 4, 2
PAD = 24
LANES = 128


def pick(table, index):
    dims = lax.GatherDimensionNumbers(
        offset_dims=(),
        collapsed_slice_dims=(0,),
        start_index_map=(0,),
        operand_batching_dims=(1,),
        start_indices_batching_dims=(1,),
    )
    rows = [
        lax.gather(
            table,
            index[8 * i : 8 * i + 8, :, None],
            dims,
            slice_sizes=(1, 1),
            mode=lax.GatherScatterMode.PROMISE_IN_BOUNDS,
        )
        for i in range(index.shape[0] // 8)
    ]
    return jnp.concatenate(rows, axis=0)


def flux(psi_up, cond_up, psi_low, cond_low):
    return (cond_up + cond_low) * (
        (psi_up - psi_low) * (0.5 * face_scale / layer_thick) + 0.5 * face_scale
    )


def kernel(
    strips, ks_hbm, al_hbm, th_hbm, p_hbm, t_hbm, a_hbm, rain_hbm, h_hbm, code_hbm, sec_hbm,
    moist, head,
    ks, al, th, pbuf, tbuf, abuf, rain, h0, code, sec, tabs, part, recv1, xs, recv2, c0, c7,
    dn_p, dn_c, up_pc, fb_out, fb_in, fa_out, fa_in,
    E, H, A, colsend, colrecv, heads,
    load_sem, misc_sem, s1_send, s1_recv, s2_send, s2_recv,
    face_send, down_recv, up_recv, fb_recv, fa_recv, col_send, col_recv, row_send, row_recv, head_send, head_recv, known,
):
    layers, rows_all, cols_all = pbuf.shape
    chunks, edges = rows_all // R, rows_all // RE
    tile = h0.shape[1]
    wide = tile + LANES
    cols_a = dn_p.shape[1]
    part_a, part_b = pl.ds(0, cols_a), pl.ds(cols_a, cols_all - cols_a)
    body = pl.ds(PAD, rows_all)
    mid, halo = pl.ds(0, tile), pl.ds(tile, LANES)
    last = layers - 1
    depth, strip = lax.axis_index("depth"), lax.axis_index("strips")
    core, chip = depth % 2, depth // 2
    mate = {"depth": chip * 2 + 1 - core}
    cross = {"depth": (depth + 2) % 4}
    above, below = {"depth": depth - 1}, {"depth": depth + 1}
    north, south = {"strips": strip - 1}, {"strips": strip + 1}
    early = edges // 3
    has_up, has_down = depth > 0, depth < 3
    has_north, has_south = strip > 0, strip < strips - 1

    def remote(src, dst, send, recv, device):
        return pltpu.make_async_remote_copy(
            src_ref=src, dst_ref=dst, send_sem=send, recv_sem=recv,
            device_id=device, device_id_type=MESH,
        )

    barrier = pltpu.get_barrier_semaphore()

    def greet(device):
        pl.semaphore_signal(barrier, inc=1, device_id=device, device_id_type=MESH)

    x, y, z, z_count = strip % XS, strip // XS % YS, strip // (XS * YS), strips // (XS * YS)
    start, end = x == 0, x == XS - 1
    corner = start & (y == 0)
    for step in (1, 2, 3):
        greet({"depth": (depth + step) % 4})
    greet({"strips": strip - x + (x + 1) % XS})
    greet({"strips": strip - x + (x + XS - 1) % XS})
    pl.when(start)(lambda: greet({"strips": strip + XS - 2 * XS * y}))
    pl.when(corner & (z > 0))(lambda: greet({"strips": strip - XS * YS}))
    pl.when(corner & (z < z_count - 1))(lambda: greet({"strips": strip + XS * YS}))
    is_start = (XS - x) // XS
    z_sides = (z + z_count - 1) // z_count + (2 * z_count - 2 - z) // z_count
    greeted = 5 + is_start + is_start * (1 - y) * z_sides

    def announce(which, target):
        pl.semaphore_signal(known.at[which], inc=1, device_id={"strips": target}, device_id_type=MESH)

    def announce_first():
        @pl.when(corner)
        def _():
            announce(0, strip + XS - 1)
            announce(0, strip + XS)
            pl.when(z < z_count - 1)(lambda: announce(1, strip + XS))

        pl.when(start & (y == 1) & (z < z_count - 1))(lambda: announce(1, strip - XS))

    def announce_second():
        @pl.when(start & (z < z_count - 1))
        def _():
            pl.semaphore_wait(known.at[1], 1)
            pl.when(y == 0)(lambda: announce(2, strip + XS * YS))
            pl.when(y == 1)(lambda: announce(2, strip + XS - 1))

    def await_announced():
        pl.when((end & (y == 0)) | (start & (y == 1)))(lambda: pl.semaphore_wait(known.at[0], 1))
        pl.when((end & (y == 1) & has_south) | (corner & has_north))(lambda: pl.semaphore_wait(known.at[2], 1))

    def load(which, chunk):
        src, dst = ((p_hbm, pbuf), (t_hbm, tbuf), (a_hbm, abuf))[which]
        where = pl.ds(pl.multiple_of(chunk * R, R), R)
        return pltpu.make_async_copy(src.at[:, where, :], dst.at[:, where, :], load_sem.at[which, chunk])

    small = [
        pltpu.make_async_copy(src, dst, misc_sem.at[i])
        for i, (src, dst) in enumerate(((h_hbm, h0), (code_hbm, code), (sec_hbm, sec), (rain_hbm, rain)))
    ]
    tables = [
        pltpu.make_async_copy(src, dst, misc_sem.at[4 + i])
        for i, (src, dst) in enumerate(((ks_hbm, ks), (al_hbm, al), (th_hbm, th)))
    ]
    for copy in tables:
        copy.start()
    for i in range(chunks):
        for which in range(3):
            load(which, (i + chunks - 1) % chunks).start()
    for copy in small:
        copy.start()

    for copy in tables:
        copy.wait()
    scales = (1.0, 0.5 * math.log2(math.e), 0.85)
    row = lax.broadcasted_iota(jnp.int32, (8, LANES), 0)
    for i, (ref, scale) in enumerate(zip((ks, al, th), scales)):
        low = high = jnp.zeros((8, LANES), jnp.float32)
        for c in range(ref.shape[0]):
            value = ref[c] * scale
            if c < 8:
                low = jnp.where(row == c, value, low)
            else:
                high = jnp.where(row == c - 8, value, high)
        tabs[i, 0] = low
        tabs[i, 1] = high

    def blank(first, count):
        for q in range(4):
            E[q, first : first + count, :] = jnp.full((count, wide), 1.0 if q == 1 else 0.0, jnp.float32)

    blank(0, PAD - 8)
    blank(PAD + rows_all + 8, PAD - 8)
    pl.when(strip == 0)(lambda: blank(PAD - 8, 8))
    pl.when(strip == strips - 1)(lambda: blank(PAD + rows_all, 8))
    for ref in (A, H):
        for q in range(ref.shape[0]):
            ref[q, 0:PAD, :] = jnp.zeros((PAD, wide), jnp.float32)
            ref[q, PAD + rows_all :, :] = jnp.zeros((PAD, wide), jnp.float32)

    def outside(side):
        group = lax.broadcasted_iota(jnp.int32, (8, LANES), 1) // 8
        for chunk in range(chunks + 1):
            colrecv[side, chunk] = jnp.where(group % 4 == 1, 1.0, 0.0)

    pl.when(depth == 0)(lambda: outside(0))
    pl.when(depth == 3)(lambda: outside(1))

    def order(i):
        return (i + chunks - 1) % chunks

    def stage1(chunk):
        return remote(
            part.at[chunk, 1 - core], recv1.at[chunk], s1_send.at[0], s1_recv.at[chunk], mate
        )

    def stage2(chunk):
        return remote(xs.at[chunk], recv2.at[chunk], s2_send.at[0], s2_recv.at[chunk], cross)

    def column_pass(chunk):
        for which in range(3):
            load(which, chunk).wait()
        where = pl.ds(pl.multiple_of(chunk * R, R), R)

        def lane_tile(block, half):
            cols = pl.ds(pl.multiple_of(block * tile + half * LANES, LANES), LANES)
            total = None
            for k in range(layers):
                p, t, a = pbuf[k, where, cols], tbuf[k, where, cols], abuf[k, where, cols]
                index, upper = t & 7, t >= 8
                sat, shape, pore = (
                    jnp.where(upper, pick(tabs[i, 1], index), pick(tabs[i, 0], index)) for i in range(3)
                )
                wet = jnp.exp2(shape * jnp.minimum(p, 0.0))
                cond = sat * (wet * wet) * a.astype(jnp.float32)
                dry = pore * (1.0 - wet)
                water = pore * (1.0 / 0.85) - dry
                charge = cond * wet
                if k == 0:
                    c0[where, cols] = cond
                    total = (cond, dry, charge)
                else:
                    total = (total[0] + cond, total[1] + dry, total[2] + charge)
                    inner = flux(p_up, cond_up, p, cond)
                    moist[k - 1, where, cols] = water_up - inner
                    water = water + inner
                p_up, cond_up, water_up = p, cond, water
            moist[last, where, cols] = water_up
            c7[where, cols] = cond_up
            for q in range(3):
                part[chunk, block % 2, block // 2, q, :, half * LANES : (half + 1) * LANES] = total[q]

        @pl.loop(0, cols_all // tile)
        def _(block):
            for half in range(tile // LANES):
                lane_tile(block, half)

    half = rows_all // 2

    def down_p(k):
        where = pl.ds(k * half, half)
        return remote(p_hbm.at[last, where, part_a], dn_p.at[where], face_send.at[0], down_recv.at[2 + k], below)

    def down_c(k):
        where = pl.ds(k * half, half)
        return remote(c7.at[where, part_a], dn_c.at[where], face_send.at[1], down_recv.at[k], below)

    def up_message(which, e):
        where = pl.ds(pl.multiple_of(e * RE, RE), RE)
        src = p_hbm.at[0, where, part_b] if which == 0 else c0.at[where, part_b]
        return remote(src, up_pc.at[e, which], face_send.at[2 + which], up_recv.at[e], above)

    def flux_down(e):
        where = pl.ds(pl.multiple_of(e * RE, RE), RE)
        return remote(fb_out.at[where], fb_in.at[where], face_send.at[4], fb_recv.at[e], below)

    def flux_up(e):
        where = pl.ds(pl.multiple_of(e * RE, RE), RE)
        return remote(fa_out.at[where], fa_in.at[where], face_send.at[5], fa_recv.at[0], above)

    def finish(chunk):
        stage2(chunk).wait_recv()
        here = pl.ds(pl.multiple_of(chunk * R, R), R)
        there = pl.ds(pl.multiple_of(PAD + chunk * R, 8), R)
        trans, store, charge = (
            (part[chunk, core, chip, q] + recv1[chunk, chip, q]) + recv2[chunk, q] for q in range(3)
        )
        store = spec_yield + store * layer_thick
        kind = code[here, :]
        river = jnp.where(kind == 1, river_cond, jnp.where(kind == 2, fixed_cond, 0.0))
        old = h0[here, :]
        root = jnp.sqrt(trans * layer_thick)
        E[0, there, mid] = root
        E[1, there, mid] = store + river
        E[2, there, mid] = store * old + charge * (leak_rate * layer_thick) + river * sec[here, :]
        E[3, there, mid] = root * old
        pack(chunk, tiles_of(chunk))

    lane = lax.broadcasted_iota(jnp.int32, (8, LANES), 1) // 8

    def column_halo(side, chunk):
        return remote(
            colsend.at[side, chunk], colrecv.at[side, chunk],
            col_send.at[side], col_recv.at[side, chunk], (below, above)[side],
        )

    def pack_tiles(side, chunk, tiles):
        edge = pl.ds(tile - LANES if side == 0 else 0, LANES)
        out = jnp.zeros((8, LANES), jnp.float32)
        for q in range(4):
            for h in range(2):
                group = q + 4 * h
                shift = (8 * group + (8 if side == 0 else 0)) % LANES
                value = E[q, tiles[h], edge]
                out = jnp.where(lane == group, pltpu.roll(value, shift, 1) if shift else value, out)
        colsend[side, chunk] = out
        column_halo(side, chunk).start()

    def tiles_of(chunk):
        return [pl.ds(pl.multiple_of(PAD + chunk * R + 8 * h, 8), 8) for h in range(2)]

    halo_tiles = [pl.ds(PAD - 8, 8), pl.ds(PAD + rows_all, 8)]

    def pack(chunk, tiles):
        pl.when(has_down)(lambda: pack_tiles(0, chunk, tiles))
        pl.when(has_up)(lambda: pack_tiles(1, chunk, tiles))

    def unpack(chunk, tiles=None):
        pl.when(has_up)(lambda: column_halo(0, chunk).wait_recv())
        pl.when(has_down)(lambda: column_halo(1, chunk).wait_recv())
        west, east = colrecv[0, chunk], colrecv[1, chunk]
        for q in range(4):
            for h in range(2):
                group = q + 4 * h
                moved = pltpu.roll(west, 120 - 8 * group, 1)
                E[q, (tiles or tiles_of(chunk))[h], halo] = jnp.where(
                    lane < 8, pltpu.roll(east, LANES - 8 * group, 1) if group else east, moved
                )

    def row_halo(side):
        mine = pl.ds(PAD if side == 0 else PAD + rows_all - 8, 8)
        theirs = pl.ds(PAD + rows_all if side == 0 else PAD - 8, 8)
        return remote(
            E.at[:, mine, mid], E.at[:, theirs, mid], row_send.at[side], row_recv.at[side], (north, south)[side]
        )

    @pl.loop(0, chunks + 2)
    def _(i):
        @pl.when(i < chunks)
        def _():
            column_pass(order(i))

        @pl.when(i == 0)
        def _():
            pl.semaphore_wait(barrier, greeted)
            announce_first()

            pl.when(has_down)(lambda: down_p(0).start())

            @pl.loop(0, early)
            def _(e):
                pl.when(has_up)(lambda: up_message(0, e).start())

        pl.when(i == chunks // 2)(announce_second)

        @pl.when(i == chunks)
        def _():
            for copy in small:
                copy.wait()

        @pl.when(i >= chunks)
        def _():
            finish(order(i - chunks))

        @pl.when(i > 1)
        def _():
            chunk = order(i - 2)
            stage1(chunk).wait_recv()
            xs[chunk] = part[chunk, core, 1 - chip] + recv1[chunk, 1 - chip]

        @pl.when(i < chunks)
        def _():
            stage1(order(i)).start()

        @pl.when(i > 1)
        def _():
            stage2(order(i - 2)).start()

    def post_faces(first, last_one):
        @pl.loop(first, last_one)
        def _(e):
            @pl.when(has_up)
            def _():
                pl.when(e >= early)(lambda: up_message(0, e).start())
                up_message(1, e).start()

    @pl.when(depth == 0)
    def _():
        moist[0] = moist[0] + face_scale * rain[...]

    def face_step(e):
        where = pl.ds(pl.multiple_of(e * RE, RE), RE)

        @pl.when(has_down)
        def _():
            remote(up_pc.at[e], up_pc.at[e], face_send.at[2], up_recv.at[e], below).wait_recv()
            value = flux(pbuf[last, where, part_b], c7[where, part_b], up_pc[e, 0], up_pc[e, 1])
            fb_out[where] = value
            moist[last, where, part_b] = moist[last, where, part_b] - value
            flux_down(e).start()

        @pl.when(has_up)
        def _():
            for k in range(2):

                @pl.when(e == k * (edges // 2))
                def _():
                    down_p(k).wait_recv()
                    down_c(k).wait_recv()

            value = flux(dn_p[where], dn_c[where], pbuf[0, where, part_a], c0[where, part_a])
            fa_out[where] = value
            moist[0, where, part_a] = moist[0, where, part_a] + value
            flux_up(e).start()

    sub = lax.broadcasted_iota(jnp.int32, (8, wide), 0)

    def rows_of(t, count=1):
        return pl.ds(pl.multiple_of(8 * t, 8), 8 * count)

    def around(ref, q, t):
        north_t, a, b, south_t = (ref[q, rows_of(t + k), :] for k in (-1, 0, 1, 2))

        def sums(before, here, after):
            down = [pltpu.roll(v, 1, 0) for v in (before, here)]
            up = [pltpu.roll(v, 7, 0) for v in (here, after)]
            return (
                pltpu.roll(here, 1, 1)
                + pltpu.roll(here, wide - 1, 1)
                + jnp.where(sub == 0, down[0], down[1])
                + jnp.where(sub == 7, up[1], up[0])
            )

        return jnp.concatenate([sums(north_t, a, b), sums(a, b, south_t)], axis=0)

    def wave(j, stages):
        at = (2 * j + 2, 2 * j, 2 * j - 3, 2 * j - 6)
        out = []
        if 3 in stages:
            here = rows_of(at[3], 2)
            out.append((H, 2, here, A[2, here, :] + A[3, here, :] * around(H, 1, at[3])))
        if 2 in stages:
            here = rows_of(at[2], 2)
            out.append((H, 1, here, A[0, here, :] + A[1, here, :] * around(H, 0, at[2])))
        if 1 in stages:
            here = rows_of(at[1], 2)
            out.append((H, 0, here, A[0, here, :] + A[1, here, :] * around(E, 3, at[1])))
        if 0 in stages:
            here = rows_of(at[0], 2)
            root = E[0, here, :]
            scale = 1.0 / (E[1, here, :] + root * around(E, 0, at[0]))
            free, bound = E[2, here, :] * scale, root * scale
            out += [(A, 0, here, root * free), (A, 1, here, root * bound), (A, 2, here, free), (A, 3, here, bound)]
        for ref, q, here, value in out:
            ref[q, here, :] = value

    def head_copy(chunk, source):
        where = pl.ds(pl.multiple_of(chunk * R, R), R)
        return remote(
            heads.at[source, where], heads.at[source, where],
            head_send.at[0], head_recv.at[source], {"depth": 3},
        )

    def hand_on(chunk):
        where = pl.ds(pl.multiple_of(chunk * R, R), R)
        value = H[SWEEPS - 1, pl.ds(pl.multiple_of(PAD + chunk * R, 8), R), mid]
        heads[depth, where] = value
        head[where, :] = value
        pl.when(depth < 3)(lambda: head_copy(chunk, depth).start())

    await_announced()
    pl.when(has_north)(lambda: row_halo(0).start())
    pl.when(has_south)(lambda: row_halo(1).start())

    def posts(down, up):
        if down is not None:
            pl.when(has_down)(lambda: down.start())
        post_faces(*up)

    finish(1)
    finish(2)
    finish(3)
    posts(down_c(0), (0, 2))
    finish(4)
    posts(None, (2, 3))
    finish(5)
    posts(down_c(1), (3, 4))
    finish(6)

    pl.when(has_south)(lambda: row_halo(0).wait_recv())
    pl.when(has_north)(lambda: row_halo(1).wait_recv())
    pack(chunks, halo_tiles)
    posts(down_p(1), (4, edges))
    face_step(0)
    face_step(1)

    @pl.loop(0, chunks - 3)
    def _(chunk):
        unpack(chunk)

    unpack(chunks - 1)
    face_step(2)
    unpack(chunks, halo_tiles)

    every = (0, 1, 2, 3)
    wave(0, (0,))
    wave(1, (0, 1))
    wave(2, (0, 1, 2))
    wave(3, (0, 1, 2))
    wave(4, (0, 1, 2, 3))
    face_step(3)

    @pl.loop(5, chunks - 1)
    def _(j):
        unpack(j)
        wave(j, every)
        hand_on(j - 5)

    face_step(4)

    @pl.loop(chunks - 1, chunks + 1)
    def _(j):
        wave(j, every)
        hand_on(j - 5)

    for j, stages in ((chunks + 1, (1, 2, 3)), (chunks + 2, (2, 3)), (chunks + 3, (2, 3)), (chunks + 4, (3,))):
        wave(j, stages)
        hand_on(j - 5)

    @pl.loop(5, edges)
    def _(e):
        face_step(e)

    @pl.when(depth == 3)
    def _():
        for block in range(4):
            if block < 3:
                remote(heads.at[block], heads.at[block], head_send.at[0], head_recv.at[block], {"depth": 0}).wait_recv()
            cols = pl.ds(block * tile, tile)
            bottom = c7[:, cols] * (
                (pbuf[last, :, cols] - heads[block]) * (2.0 * face_scale / layer_thick) + face_scale
            )
            moist[last, :, cols] = moist[last, :, cols] - bottom

    @pl.when(has_down)
    def _():
        remote(fa_in, fa_in, face_send.at[5], fa_recv.at[0], below).wait_recv()
        moist[last, :, part_a] = moist[last, :, part_a] - fa_in[...]

    @pl.when(has_up)
    def _():
        @pl.loop(0, edges)
        def _(e):
            where = pl.ds(pl.multiple_of(e * RE, RE), RE)
            flux_down(e).wait_recv()
            moist[0, where, part_b] = moist[0, where, part_b] + fb_in[where]

    remote(part.at[:, 1 - core], recv1, s1_send.at[0], s1_recv.at[0], mate).wait_send()
    remote(xs, recv2, s2_send.at[0], s2_recv.at[0], cross).wait_send()

    @pl.when(has_down)
    def _():
        remote(p_hbm.at[last, :, part_a], dn_p, face_send.at[0], down_recv.at[2], below).wait_send()
        remote(c7.at[:, part_a], dn_c, face_send.at[1], down_recv.at[1], below).wait_send()
        remote(fb_out, fb_in, face_send.at[4], fb_recv.at[0], below).wait_send()
        remote(colsend.at[0], colrecv.at[0], col_send.at[0], col_recv.at[0, 0], below).wait_send()
        remote(heads.at[depth], heads.at[depth], head_send.at[0], head_recv.at[depth], {"depth": 3}).wait_send()

    @pl.when(has_up)
    def _():
        remote(p_hbm.at[0, :, part_b], fb_in, face_send.at[2], up_recv.at[0], above).wait_send()
        remote(c0.at[:, part_b], fb_in, face_send.at[3], up_recv.at[0], above).wait_send()
        remote(fa_out, fa_in, face_send.at[5], fa_recv.at[0], above).wait_send()
        remote(colsend.at[1], colrecv.at[1], col_send.at[1], col_recv.at[1, 0], above).wait_send()

    pl.when(has_north)(lambda: row_halo(0).wait_send())
    pl.when(has_south)(lambda: row_halo(1).wait_send())


def store_kernel(moist, head, moist_out, head_out, sems):
    copies = [pltpu.make_async_copy(head, head_out, sems.at[0])]
    for k in range(moist.shape[0]):
        copies.append(pltpu.make_async_copy(moist.at[k], moist_out.at[k], sems.at[k + 1]))
    for copy in copies:
        copy.start()
    for copy in copies:
        copy.wait()


def shards(strips, pressure, texture, active, rain, k_sat, alpha, theta_sat, head_old, cell_code, section):
    layers, rows, cols = pressure.shape
    tile = head_old.shape[1]
    wide = tile + LANES
    cols_a = 3 * LANES
    cols_b = cols - cols_a
    chunks, edges = rows // R, rows // RE
    f32 = jnp.float32
    vmem = lambda *shape: pltpu.VMEM(shape, f32)
    dma = lambda *shape: pltpu.SemaphoreType.DMA(shape)
    table = pltpu.SMEM(k_sat.shape, f32)
    scratch = [
        table,
        table,
        table,
        vmem(layers, rows, cols),
        pltpu.VMEM((layers, rows, cols), jnp.int32),
        pltpu.VMEM((layers, rows, cols), jnp.int32),
        vmem(rows, cols),
        vmem(rows, tile),
        pltpu.VMEM((rows, tile), jnp.int32),
        vmem(rows, tile),
        vmem(3, 2, 8, LANES),
        vmem(chunks, 2, 2, 3, R, tile),
        vmem(chunks, 2, 3, R, tile),
        vmem(chunks, 3, R, tile),
        vmem(chunks, 3, R, tile),
        vmem(rows, cols),
        vmem(rows, cols),
        vmem(rows, cols_a),
        vmem(rows, cols_a),
        vmem(edges, 2, RE, cols_b),
        vmem(rows, cols_b),
        vmem(rows, cols_b),
        vmem(rows, cols_a),
        vmem(rows, cols_a),
        vmem(4, rows + 2 * PAD, wide),
        vmem(SWEEPS, rows + 2 * PAD, wide),
        vmem(4, rows + 2 * PAD, wide),
        vmem(2, chunks + 1, 8, LANES),
        vmem(2, chunks + 1, 8, LANES),
        vmem(4, rows, tile),
        dma(3, chunks),
        dma(7),
        dma(1),
        dma(chunks),
        dma(1),
        dma(chunks),
        dma(6),
        dma(4),
        dma(edges),
        dma(edges),
        dma(1),
        dma(2),
        dma(2, chunks + 1),
        dma(2),
        dma(2),
        dma(1),
        dma(4),
        pltpu.SemaphoreType.REGULAR((3,)),
    ]
    anywhere = pl.BlockSpec(memory_space=pltpu.HBM)
    moist, head = pl.pallas_call(
        functools.partial(kernel, strips),
        out_shape=(
            pltpu.VMEM((layers, rows, cols), f32),
            pltpu.VMEM((rows, tile), f32),
        ),
        in_specs=[anywhere] * 10,
        out_specs=(pl.BlockSpec(memory_space=pltpu.VMEM), pl.BlockSpec(memory_space=pltpu.VMEM)),
        scratch_shapes=scratch,
        compiler_params=pltpu.CompilerParams(
            collective_id=0, has_side_effects=True, vmem_limit_bytes=59 * 2**20
        ),
        name="soil_column",
    )(k_sat, alpha, theta_sat, pressure, texture, active, rain, head_old, cell_code, section)
    on_chip = pl.BlockSpec(memory_space=pltpu.VMEM)
    return pl.pallas_call(
        store_kernel,
        out_shape=(
            jax.ShapeDtypeStruct((layers, rows, cols), f32),
            jax.ShapeDtypeStruct((rows, tile), f32),
        ),
        in_specs=[on_chip] * 2,
        out_specs=(anywhere, anywhere),
        scratch_shapes=[dma(layers + 1)],
        compiler_params=pltpu.CompilerParams(vmem_limit_bytes=2**20),
        name="store",
    )(pltpu.with_memory_space_constraint(moist, pltpu.VMEM), pltpu.with_memory_space_constraint(head, pltpu.VMEM))


def solution(mesh):
    in_specs = (
        P("depth", "strips", None),
        P("depth", "strips", None),
        P("depth", "strips", None),
        P("strips", None),
        P(),
        P(),
        P(),
        P("strips", "depth"),
        P("strips", "depth"),
        P("strips", "depth"),
    )
    out_specs = (P("depth", "strips", None), P("strips", "depth"))
    body = functools.partial(shards, mesh.shape["strips"])
    return jax.shard_map(body, mesh=mesh, in_specs=in_specs, out_specs=out_specs, check_vma=False)
```

```python
import functools
import math

import jax
import jax.numpy as jnp
from jax import lax
from jax.experimental import pallas as pl
from jax.experimental.pallas import tpu as pltpu
from jax.sharding import PartitionSpec as P

MESH = pl.DeviceIdType.MESH
SWEEPS = 3

layer_thick = 0.05
soil_step = 0.0002
spec_yield = 0.02
leak_rate = 0.5
river_cond = 0.5
fixed_cond = 3.0
face_scale = soil_step / layer_thick

R = 16
RE = R
EARLY = 4
XS, YS = 4, 2
PAD = 24
LANES = 128


def pick(table, index):
    dims = lax.GatherDimensionNumbers(
        offset_dims=(),
        collapsed_slice_dims=(0,),
        start_index_map=(0,),
        operand_batching_dims=(1,),
        start_indices_batching_dims=(1,),
    )
    rows = [
        lax.gather(
            table,
            index[8 * i : 8 * i + 8, :, None],
            dims,
            slice_sizes=(1, 1),
            mode=lax.GatherScatterMode.PROMISE_IN_BOUNDS,
        )
        for i in range(index.shape[0] // 8)
    ]
    return jnp.concatenate(rows, axis=0)


def flux(psi_up, cond_up, psi_low, cond_low):
    return (cond_up + cond_low) * (
        (psi_up - psi_low) * (0.5 * face_scale / layer_thick) + 0.5 * face_scale
    )


def kernel(
    strips, ks_hbm, al_hbm, th_hbm, p_hbm, t_hbm, a_hbm, rain_hbm, h_hbm, code_hbm, sec_hbm,
    moist, head,
    ks, al, th, pbuf, tbuf, abuf, rain, h0, code, sec, tabs, part, recv1, xs, recv2, c0, c7,
    dn_p, dn_c, up_pc, fb_out, fb_in, fa_out, fa_in,
    E, H, A, colsend, colrecv, heads, rowsend, rowrecv,
    load_sem, misc_sem, s1_send, s1_recv, s2_send, s2_recv,
    face_send, down_recv, up_recv, fb_recv, fa_recv, col_send, col_recv, row_send, row_recv, head_send, head_recv, known,
):
    layers, rows_all, cols_all = pbuf.shape
    chunks, edges = rows_all // R, rows_all // RE
    tile = h0.shape[1]
    wide = tile + LANES
    cols_a = dn_p.shape[1]
    part_a, part_b = pl.ds(0, cols_a), pl.ds(cols_a, cols_all - cols_a)
    body = pl.ds(PAD, rows_all)
    mid, halo = pl.ds(0, tile), pl.ds(tile, LANES)
    last = layers - 1
    depth, strip = lax.axis_index("depth"), lax.axis_index("strips")
    core, chip = depth % 2, depth // 2
    mate = {"depth": chip * 2 + 1 - core}
    cross = {"depth": (depth + 2) % 4}
    above, below = {"depth": depth - 1}, {"depth": depth + 1}
    north, south = {"strips": strip - 1}, {"strips": strip + 1}
    has_up, has_down = depth > 0, depth < 3
    has_north, has_south = strip > 0, strip < strips - 1

    def remote(src, dst, send, recv, device):
        return pltpu.make_async_remote_copy(
            src_ref=src, dst_ref=dst, send_sem=send, recv_sem=recv,
            device_id=device, device_id_type=MESH,
        )

    barrier = pltpu.get_barrier_semaphore()

    def greet(device):
        pl.semaphore_signal(barrier, inc=1, device_id=device, device_id_type=MESH)

    x, y, z, z_count = strip % XS, strip // XS % YS, strip // (XS * YS), strips // (XS * YS)
    start, end = x == 0, x == XS - 1
    corner = start & (y == 0)
    for step in (1, 2, 3):
        greet({"depth": (depth + step) % 4})
    greet({"strips": strip - x + (x + 1) % XS})
    greet({"strips": strip - x + (x + XS - 1) % XS})
    pl.when(start)(lambda: greet({"strips": strip + XS - 2 * XS * y}))
    pl.when(corner & (z > 0))(lambda: greet({"strips": strip - XS * YS}))
    pl.when(corner & (z < z_count - 1))(lambda: greet({"strips": strip + XS * YS}))
    is_start = (XS - x) // XS
    z_sides = (z + z_count - 1) // z_count + (2 * z_count - 2 - z) // z_count
    greeted = 5 + is_start + is_start * (1 - y) * z_sides

    def announce(which, target):
        pl.semaphore_signal(known.at[which], inc=1, device_id={"strips": target}, device_id_type=MESH)

    def announce_first():
        @pl.when(corner)
        def _():
            announce(0, strip + XS - 1)
            announce(0, strip + XS)
            pl.when(z < z_count - 1)(lambda: announce(1, strip + XS))

        pl.when(start & (y == 1) & (z < z_count - 1))(lambda: announce(1, strip - XS))

    def announce_second():
        @pl.when(start & (z < z_count - 1))
        def _():
            pl.semaphore_wait(known.at[1], 1)
            pl.when(y == 0)(lambda: announce(2, strip + XS * YS))
            pl.when(y == 1)(lambda: announce(2, strip + XS - 1))

    def await_announced():
        pl.when((end & (y == 0)) | (start & (y == 1)))(lambda: pl.semaphore_wait(known.at[0], 1))
        pl.when((end & (y == 1) & has_south) | (corner & has_north))(lambda: pl.semaphore_wait(known.at[2], 1))

    def load(which, chunk):
        src, dst = ((p_hbm, pbuf), (t_hbm, tbuf), (a_hbm, abuf))[which]
        where = pl.ds(pl.multiple_of(chunk * R, R), R)
        return pltpu.make_async_copy(src.at[:, where, :], dst.at[:, where, :], load_sem.at[chunk])

    small = [
        pltpu.make_async_copy(src, dst, misc_sem.at[0])
        for i, (src, dst) in enumerate(((h_hbm, h0), (code_hbm, code), (sec_hbm, sec), (rain_hbm, rain)))
    ]
    tables = [
        pltpu.make_async_copy(src, dst, misc_sem.at[1 + i])
        for i, (src, dst) in enumerate(((ks_hbm, ks), (al_hbm, al), (th_hbm, th)))
    ]
    for copy in tables:
        copy.start()
    for i in range(chunks):
        for which in range(3):
            load(which, (i + chunks - 1) % chunks).start()
    for copy in small:
        copy.start()

    for copy in tables:
        copy.wait()
    scales = (1.0, 0.5 * math.log2(math.e), 0.85)
    row = lax.broadcasted_iota(jnp.int32, (8, LANES), 0)
    for i, (ref, scale) in enumerate(zip((ks, al, th), scales)):
        low = high = jnp.zeros((8, LANES), jnp.float32)
        for c in range(ref.shape[0]):
            value = ref[c] * scale
            if c < 8:
                low = jnp.where(row == c, value, low)
            else:
                high = jnp.where(row == c - 8, value, high)
        tabs[i, 0] = low
        tabs[i, 1] = high

    def blank(first, count):
        for q in range(4):
            E[q, first : first + count, :] = jnp.full((count, wide), 1.0 if q == 1 else 0.0, jnp.float32)

    blank(0, PAD - 8)
    blank(PAD + rows_all + 8, PAD - 8)
    pl.when(strip == 0)(lambda: blank(PAD - 8, 8))
    pl.when(strip == strips - 1)(lambda: blank(PAD + rows_all, 8))
    for ref in (A, H):
        for q in range(ref.shape[0]):
            ref[q, 0:PAD, :] = jnp.zeros((PAD, wide), jnp.float32)
            ref[q, PAD + rows_all :, :] = jnp.zeros((PAD, wide), jnp.float32)

    def outside(side):
        group = lax.broadcasted_iota(jnp.int32, (8, LANES), 1) // 8
        for chunk in range(chunks + 1):
            colrecv[side, chunk] = jnp.where(group % 4 == 1, 1.0, 0.0)

    pl.when(depth == 0)(lambda: outside(0))
    pl.when(depth == 3)(lambda: outside(1))

    def order(i):
        return (i + chunks - 1) % chunks

    def stage1(chunk):
        return remote(
            part.at[chunk, 1 - core], recv1.at[chunk], s1_send.at[0], s1_recv.at[chunk], mate
        )

    def stage2(chunk):
        return remote(xs.at[chunk], recv2.at[chunk], s2_send.at[0], s2_recv.at[chunk], cross)

    def column_pass(chunk):
        where = pl.ds(pl.multiple_of(chunk * R, R), R)

        def lane_tile(block, half):
            cols = pl.ds(pl.multiple_of(block * tile + half * LANES, LANES), LANES)
            total = None
            for k in range(layers):
                p, t, a = pbuf[k, where, cols], tbuf[k, where, cols], abuf[k, where, cols]
                index, upper = t & 7, t >= 8
                sat, shape, pore = (
                    jnp.where(upper, pick(tabs[i, 1], index), pick(tabs[i, 0], index)) for i in range(3)
                )
                wet = jnp.exp2(shape * jnp.minimum(p, 0.0))
                cond = sat * (wet * wet) * a.astype(jnp.float32)
                dry = pore * (1.0 - wet)
                water = pore * (1.0 / 0.85) - dry
                charge = cond * wet
                if k == 0:
                    c0[where, cols] = cond
                    total = (cond, dry, charge)
                else:
                    total = (total[0] + cond, total[1] + dry, total[2] + charge)
                    inner = flux(p_up, cond_up, p, cond)
                    moist[k - 1, where, cols] = water_up - inner
                    water = water + inner
                p_up, cond_up, water_up = p, cond, water
            moist[last, where, cols] = water_up
            c7[where, cols] = cond_up
            for q in range(3):
                part[chunk, block % 2, block // 2, q, :, half * LANES : (half + 1) * LANES] = total[q]

        @pl.loop(0, cols_all // tile)
        def _(block):
            for half in range(tile // LANES):
                lane_tile(block, half)

    half = rows_all // 2

    def down_p(e):
        where = pl.ds(pl.multiple_of(e * RE, RE), RE)
        k = e // (edges // 2)
        return remote(pbuf.at[last, where, part_a], dn_p.at[where], face_send.at[0], down_recv.at[2 + k], below)

    def down_c(k):
        where = pl.ds(k * half, half)
        return remote(c7.at[where, part_a], dn_c.at[where], face_send.at[1], down_recv.at[k], below)

    def up_message(which, e):
        where = pl.ds(pl.multiple_of(e * RE, RE), RE)
        src = (pbuf.at[0, where, part_b], c0.at[where, part_b])[which]
        return remote(src, up_pc.at[e, which], face_send.at[2 + which], up_recv.at[e], above)

    def flux_down(e):
        where = pl.ds(pl.multiple_of(e * RE, RE), RE)
        return remote(fb_out.at[where], fb_in.at[where], face_send.at[4], fb_recv.at[0], below)

    def flux_up(e):
        where = pl.ds(pl.multiple_of(e * RE, RE), RE)
        return remote(fa_out.at[where], fa_in.at[where], face_send.at[5], fa_recv.at[0], above)

    def finish(chunk):
        stage2(chunk).wait_recv()
        here = pl.ds(pl.multiple_of(chunk * R, R), R)
        there = pl.ds(pl.multiple_of(PAD + chunk * R, 8), R)
        trans, store, charge = (
            (part[chunk, core, chip, q] + recv1[chunk, chip, q]) + recv2[chunk, q] for q in range(3)
        )
        store = spec_yield + store * layer_thick
        kind = code[here, :]
        river = jnp.where(kind == 1, river_cond, jnp.where(kind == 2, fixed_cond, 0.0))
        old = h0[here, :]
        root = jnp.sqrt(trans * layer_thick)
        E[0, there, mid] = root
        E[1, there, mid] = store + river
        E[2, there, mid] = store * old + charge * (leak_rate * layer_thick) + river * sec[here, :]
        E[3, there, mid] = root * old
        pack(chunk, tiles_of(chunk))

    lane = lax.broadcasted_iota(jnp.int32, (8, LANES), 1) // 8

    def column_halo(side, chunk):
        return remote(
            colsend.at[side, chunk], colrecv.at[side, chunk],
            col_send.at[side], col_recv.at[chunk], (below, above)[side],
        )

    def pack_tiles(side, chunk, tiles):
        edge = pl.ds(tile - LANES if side == 0 else 0, LANES)
        out = jnp.zeros((8, LANES), jnp.float32)
        for q in range(4):
            for h in range(2):
                group = q + 4 * h
                shift = (8 * group + (8 if side == 0 else 0)) % LANES
                value = E[q, tiles[h], edge]
                out = jnp.where(lane == group, pltpu.roll(value, shift, 1) if shift else value, out)
        colsend[side, chunk] = out
        column_halo(side, chunk).start()

    def tiles_of(chunk):
        return [pl.ds(pl.multiple_of(PAD + chunk * R + 8 * h, 8), 8) for h in range(2)]

    halo_tiles = [pl.ds(PAD - 8, 8), pl.ds(PAD + rows_all, 8)]

    def pack(chunk, tiles):
        pl.when(has_down)(lambda: pack_tiles(0, chunk, tiles))
        pl.when(has_up)(lambda: pack_tiles(1, chunk, tiles))

    def unpack(chunk, tiles=None):
        pl.when(depth == 0)(lambda: column_halo(1, chunk).wait_recv())
        pl.when(depth == 3)(lambda: column_halo(0, chunk).wait_recv())

        @pl.when(has_up & has_down)
        def _():
            remote(
                colsend.at[:, chunk], colrecv.at[:, chunk], col_send.at[0], col_recv.at[chunk], below
            ).wait_recv()

        west, east = colrecv[0, chunk], colrecv[1, chunk]
        for q in range(4):
            for h in range(2):
                group = q + 4 * h
                moved = pltpu.roll(west, 120 - 8 * group, 1)
                E[q, (tiles or tiles_of(chunk))[h], halo] = jnp.where(
                    lane < 8, pltpu.roll(east, LANES - 8 * group, 1) if group else east, moved
                )

    row8 = lax.broadcasted_iota(jnp.int32, (8, LANES), 0)
    turns = ((0, 3, 6, 0, 2), (3, 6, 0, 2, 4))

    def turned(value, shift):
        return pltpu.roll(value, shift % 8, 0) if shift % 8 else value

    def row_halo(side):
        return remote(rowsend.at[side], rowrecv.at[side], row_send.at[side], row_recv.at[side], (north, south)[side])

    def send_rows(side):
        mine = pl.ds(PAD if side == 0 else PAD + rows_all - 8, 8)
        for k in range(2):
            cols = pl.ds(k * LANES, LANES)
            root, product, base = (turned(E[q, mine, cols], turns[side][n]) for n, q in enumerate((0, 3, 1)))
            rowsend[side, :, cols] = jnp.where(row8 < 3, root, jnp.where(row8 < 6, product, base))
        first, second = (turned(E[2, mine, pl.ds(k * LANES, LANES)], turns[side][3 + k]) for k in range(2))
        rowsend[side, :, 2 * LANES :] = jnp.where(row8 < 2, first, second)
        row_halo(side).start()

    def take_rows(side):
        row_halo(side).wait_recv()
        theirs = pl.ds(PAD + rows_all if side == 0 else PAD - 8, 8)
        for k in range(2):
            cols = pl.ds(k * LANES, LANES)
            value = rowrecv[side, :, cols]
            for n, q in enumerate((0, 3, 1)):
                E[q, theirs, cols] = turned(value, 8 - turns[side][n])
            E[2, theirs, cols] = turned(rowrecv[side, :, 2 * LANES :], 8 - turns[side][3 + k])

    @pl.loop(0, chunks + 2)
    def _(i):
        @pl.when(i < chunks)
        def _():
            three = pl.ds(0, 3 * R)
            pltpu.make_async_copy(p_hbm.at[:, three, :], pbuf.at[:, three, :], load_sem.at[order(i)]).wait()

        @pl.when(i == 0)
        def _():
            pl.semaphore_wait(barrier, greeted)
            announce_first()

        @pl.when(i < EARLY)
        def _():
            pl.when(has_down)(lambda: down_p(order(i)).start())
            pl.when(has_up)(lambda: up_message(0, order(i)).start())

        @pl.when(i < chunks)
        def _():
            column_pass(order(i))

        pl.when(i == chunks // 2)(announce_second)

        @pl.when(i == chunks)
        def _():
            seven = pl.ds(0, 3 + cols_all // tile)
            pltpu.make_async_copy(p_hbm.at[seven, :, mid], pbuf.at[seven, :, mid], misc_sem.at[0]).wait()

        @pl.when(i >= chunks)
        def _():
            finish(order(i - chunks))

        @pl.when(i > 1)
        def _():
            chunk = order(i - 2)
            stage1(chunk).wait_recv()
            xs[chunk] = part[chunk, core, 1 - chip] + recv1[chunk, 1 - chip]

        @pl.when(i < chunks)
        def _():
            stage1(order(i)).start()

        @pl.when(i > 1)
        def _():
            stage2(order(i - 2)).start()

    def post_faces(first, last_one):
        @pl.loop(first, last_one)
        def _(e):
            @pl.when(has_up)
            def _():
                pl.when((e >= EARLY - 1) & (e < edges - 1))(lambda: up_message(0, e).start())
                up_message(1, e).start()

    @pl.when(depth == 0)
    def _():
        moist[0] = moist[0] + face_scale * rain[...]

    def face_step(e):
        where = pl.ds(pl.multiple_of(e * RE, RE), RE)

        @pl.when(has_down)
        def _():
            remote(up_pc.at[e], up_pc.at[e], face_send.at[2], up_recv.at[e], below).wait_recv()
            value = flux(pbuf[last, where, part_b], c7[where, part_b], up_pc[e, 0], up_pc[e, 1])
            fb_out[where] = value
            moist[last, where, part_b] = moist[last, where, part_b] - value
            flux_down(e).start()

        @pl.when(has_up)
        def _():
            for k in range(2):

                @pl.when(e == k * (edges // 2))
                def _():
                    where = pl.ds(k * half, half)
                    remote(dn_p.at[where], dn_p.at[where], face_send.at[0], down_recv.at[2 + k], above).wait_recv()
                    down_c(k).wait_recv()

            value = flux(dn_p[where], dn_c[where], pbuf[0, where, part_a], c0[where, part_a])
            fa_out[where] = value
            moist[0, where, part_a] = moist[0, where, part_a] + value
            flux_up(e).start()

    sub = lax.broadcasted_iota(jnp.int32, (8, wide), 0)

    def rows_of(t, count=1):
        return pl.ds(pl.multiple_of(8 * t, 8), 8 * count)

    def around(ref, q, t):
        north_t, a, b, south_t = (ref[q, rows_of(t + k), :] for k in (-1, 0, 1, 2))

        def sums(before, here, after):
            down = [pltpu.roll(v, 1, 0) for v in (before, here)]
            up = [pltpu.roll(v, 7, 0) for v in (here, after)]
            return (
                pltpu.roll(here, 1, 1)
                + pltpu.roll(here, wide - 1, 1)
                + jnp.where(sub == 0, down[0], down[1])
                + jnp.where(sub == 7, up[1], up[0])
            )

        return jnp.concatenate([sums(north_t, a, b), sums(a, b, south_t)], axis=0)

    def wave(j, stages):
        at = (2 * j + 2, 2 * j, 2 * j - 3, 2 * j - 6)
        out = []
        if 3 in stages:
            here = rows_of(at[3], 2)
            out.append((H, 2, here, A[2, here, :] + A[3, here, :] * around(H, 1, at[3])))
        if 2 in stages:
            here = rows_of(at[2], 2)
            out.append((H, 1, here, A[0, here, :] + A[1, here, :] * around(H, 0, at[2])))
        if 1 in stages:
            here = rows_of(at[1], 2)
            out.append((H, 0, here, A[0, here, :] + A[1, here, :] * around(E, 3, at[1])))
        if 0 in stages:
            here = rows_of(at[0], 2)
            root = E[0, here, :]
            scale = 1.0 / (E[1, here, :] + root * around(E, 0, at[0]))
            free, bound = E[2, here, :] * scale, root * scale
            out += [(A, 0, here, root * free), (A, 1, here, root * bound), (A, 2, here, free), (A, 3, here, bound)]
        for ref, q, here, value in out:
            ref[q, here, :] = value

    def head_copy(chunk, source):
        where = pl.ds(pl.multiple_of(chunk * R, R), R)
        return remote(
            heads.at[source, where], heads.at[source, where],
            head_send.at[0], head_recv.at[source], {"depth": 3},
        )

    def hand_on(chunk):
        where = pl.ds(pl.multiple_of(chunk * R, R), R)
        value = H[SWEEPS - 1, pl.ds(pl.multiple_of(PAD + chunk * R, 8), R), mid]
        heads[depth, where] = value
        head[where, :] = value
        pl.when(depth < 3)(lambda: head_copy(chunk, depth).start())

    await_announced()
    pl.when(has_north)(lambda: send_rows(0))
    pl.when(has_south)(lambda: send_rows(1))

    def posts(down, up):
        for copy in down:
            pl.when(has_down)(copy)
        post_faces(*up)

    finish(1)
    finish(2)
    finish(3)
    posts([lambda: down_c(0).start()], (0, 2))
    finish(4)
    posts([lambda: down_p(EARLY - 1).start()], (2, 3))
    finish(5)
    posts([lambda: down_c(1).start()], (3, 4))
    finish(6)

    pl.when(has_south)(lambda: take_rows(0))
    pl.when(has_north)(lambda: take_rows(1))
    pack(chunks, halo_tiles)
    posts([lambda e=e: down_p(e).start() for e in range(EARLY, edges - 1)], (4, edges))
    face_step(0)
    face_step(1)

    @pl.loop(0, chunks - 3)
    def _(chunk):
        unpack(chunk)

    unpack(chunks - 1)
    face_step(2)
    unpack(chunks, halo_tiles)

    every = (0, 1, 2, 3)
    wave(0, (0,))
    wave(1, (0, 1))
    wave(2, (0, 1, 2))
    wave(3, (0, 1, 2))
    wave(4, (0, 1, 2, 3))
    face_step(3)

    @pl.loop(5, chunks - 1)
    def _(j):
        unpack(j)
        wave(j, every)
        hand_on(j - 5)

    face_step(4)

    @pl.loop(chunks - 1, chunks + 1)
    def _(j):
        wave(j, every)
        hand_on(j - 5)

    for j, stages in ((chunks + 1, (1, 2, 3)), (chunks + 2, (2, 3)), (chunks + 3, (2, 3)), (chunks + 4, (3,))):
        wave(j, stages)
        hand_on(j - 5)

    @pl.loop(5, edges)
    def _(e):
        face_step(e)

    @pl.when(depth == 3)
    def _():
        for block in range(4):
            if block < 3:
                remote(heads.at[block], heads.at[block], head_send.at[0], head_recv.at[block], {"depth": 0}).wait_recv()
            cols = pl.ds(block * tile, tile)
            bottom = c7[:, cols] * (
                (pbuf[last, :, cols] - heads[block]) * (2.0 * face_scale / layer_thick) + face_scale
            )
            moist[last, :, cols] = moist[last, :, cols] - bottom

    @pl.when(has_down)
    def _():
        remote(fa_in, fa_in, face_send.at[5], fa_recv.at[0], below).wait_recv()
        moist[last, :, part_a] = moist[last, :, part_a] - fa_in[...]

    @pl.when(has_up)
    def _():
        remote(fb_in, fb_in, face_send.at[4], fb_recv.at[0], above).wait_recv()
        moist[0, :, part_b] = moist[0, :, part_b] + fb_in[...]

    remote(part.at[:, 1 - core], recv1, s1_send.at[0], s1_recv.at[0], mate).wait_send()
    remote(xs, recv2, s2_send.at[0], s2_recv.at[0], cross).wait_send()

    @pl.when(has_down)
    def _():
        remote(c7.at[:, part_a], dn_p, face_send.at[0], down_recv.at[2], below).wait_send()
        remote(c7.at[:, part_a], dn_c, face_send.at[1], down_recv.at[1], below).wait_send()
        remote(fb_out, fb_in, face_send.at[4], fb_recv.at[0], below).wait_send()
        remote(colsend.at[0], colrecv.at[0], col_send.at[0], col_recv.at[0], below).wait_send()
        remote(heads.at[depth], heads.at[depth], head_send.at[0], head_recv.at[depth], {"depth": 3}).wait_send()

    @pl.when(has_up)
    def _():
        remote(c0.at[:, part_b], fb_in, face_send.at[2], up_recv.at[0], above).wait_send()
        remote(c0.at[:, part_b], fb_in, face_send.at[3], up_recv.at[0], above).wait_send()
        remote(fa_out, fa_in, face_send.at[5], fa_recv.at[0], above).wait_send()
        remote(colsend.at[1], colrecv.at[1], col_send.at[1], col_recv.at[0], above).wait_send()

    pl.when(has_north)(lambda: row_halo(0).wait_send())
    pl.when(has_south)(lambda: row_halo(1).wait_send())


def store_kernel(moist, head, moist_out, head_out, sems):
    copies = [pltpu.make_async_copy(head, head_out, sems.at[0])]
    for k in range(moist.shape[0]):
        copies.append(pltpu.make_async_copy(moist.at[k], moist_out.at[k], sems.at[k + 1]))
    for copy in copies:
        copy.start()
    for copy in copies:
        copy.wait()


def shards(strips, pressure, texture, active, rain, k_sat, alpha, theta_sat, head_old, cell_code, section):
    layers, rows, cols = pressure.shape
    tile = head_old.shape[1]
    wide = tile + LANES
    cols_a = 3 * LANES
    cols_b = cols - cols_a
    chunks, edges = rows // R, rows // RE
    f32 = jnp.float32
    vmem = lambda *shape: pltpu.VMEM(shape, f32)
    dma = lambda *shape: pltpu.SemaphoreType.DMA(shape)
    table = pltpu.SMEM(k_sat.shape, f32)
    scratch = [
        table,
        table,
        table,
        vmem(layers, rows, cols),
        pltpu.VMEM((layers, rows, cols), jnp.int32),
        pltpu.VMEM((layers, rows, cols), jnp.int32),
        vmem(rows, cols),
        vmem(rows, tile),
        pltpu.VMEM((rows, tile), jnp.int32),
        vmem(rows, tile),
        vmem(3, 2, 8, LANES),
        vmem(chunks, 2, 2, 3, R, tile),
        vmem(chunks, 2, 3, R, tile),
        vmem(chunks, 3, R, tile),
        vmem(chunks, 3, R, tile),
        vmem(rows, cols),
        vmem(rows, cols),
        vmem(rows, cols_a),
        vmem(rows, cols_a),
        vmem(edges, 2, RE, cols_b),
        vmem(rows, cols_b),
        vmem(rows, cols_b),
        vmem(rows, cols_a),
        vmem(rows, cols_a),
        vmem(4, rows + 2 * PAD, wide),
        vmem(SWEEPS, rows + 2 * PAD, wide),
        vmem(4, rows + 2 * PAD, wide),
        vmem(2, chunks + 1, 8, LANES),
        vmem(2, chunks + 1, 8, LANES),
        vmem(4, rows, tile),
        vmem(2, 8, 3 * LANES),
        vmem(2, 8, 3 * LANES),
        dma(chunks),
        dma(4),
        dma(1),
        dma(chunks),
        dma(1),
        dma(chunks),
        dma(6),
        dma(4),
        dma(edges),
        dma(1),
        dma(1),
        dma(2),
        dma(chunks + 1),
        dma(2),
        dma(2),
        dma(1),
        dma(4),
        pltpu.SemaphoreType.REGULAR((3,)),
    ]
    anywhere = pl.BlockSpec(memory_space=pltpu.HBM)
    moist, head = pl.pallas_call(
        functools.partial(kernel, strips),
        out_shape=(
            pltpu.VMEM((layers, rows, cols), f32),
            pltpu.VMEM((rows, tile), f32),
        ),
        in_specs=[anywhere] * 10,
        out_specs=(pl.BlockSpec(memory_space=pltpu.VMEM), pl.BlockSpec(memory_space=pltpu.VMEM)),
        scratch_shapes=scratch,
        compiler_params=pltpu.CompilerParams(
            collective_id=0, has_side_effects=True, vmem_limit_bytes=59 * 2**20
        ),
        name="soil_column",
    )(k_sat, alpha, theta_sat, pressure, texture, active, rain, head_old, cell_code, section)
    on_chip = pl.BlockSpec(memory_space=pltpu.VMEM)
    return pl.pallas_call(
        store_kernel,
        out_shape=(
            jax.ShapeDtypeStruct((layers, rows, cols), f32),
            jax.ShapeDtypeStruct((rows, tile), f32),
        ),
        in_specs=[on_chip] * 2,
        out_specs=(anywhere, anywhere),
        scratch_shapes=[dma(layers + 1)],
        compiler_params=pltpu.CompilerParams(vmem_limit_bytes=2**20),
        name="store",
    )(pltpu.with_memory_space_constraint(moist, pltpu.VMEM), pltpu.with_memory_space_constraint(head, pltpu.VMEM))


def solution(mesh):
    in_specs = (
        P("depth", "strips", None),
        P("depth", "strips", None),
        P("depth", "strips", None),
        P("strips", None),
        P(),
        P(),
        P(),
        P("strips", "depth"),
        P("strips", "depth"),
        P("strips", "depth"),
    )
    out_specs = (P("depth", "strips", None), P("strips", "depth"))
    body = functools.partial(shards, mesh.shape["strips"])
    return jax.shard_map(body, mesh=mesh, in_specs=in_specs, out_specs=out_specs, check_vma=False)
```

```python
import functools
import math

import jax
import jax.numpy as jnp
from jax import lax
from jax.experimental import pallas as pl
from jax.experimental.pallas import tpu as pltpu
from jax.sharding import PartitionSpec as P

MESH = pl.DeviceIdType.MESH
SWEEPS = 3

layer_thick = 0.05
soil_step = 0.0002
spec_yield = 0.02
leak_rate = 0.5
river_cond = 0.5
fixed_cond = 3.0
face_scale = soil_step / layer_thick

R = 16
RE = R
EARLY = 4
XS, YS = 4, 2
PAD = 24
LANES = 128


def pick(table, index):
    dims = lax.GatherDimensionNumbers(
        offset_dims=(),
        collapsed_slice_dims=(0,),
        start_index_map=(0,),
        operand_batching_dims=(1,),
        start_indices_batching_dims=(1,),
    )
    rows = [
        lax.gather(
            table,
            index[8 * i : 8 * i + 8, :, None],
            dims,
            slice_sizes=(1, 1),
            mode=lax.GatherScatterMode.PROMISE_IN_BOUNDS,
        )
        for i in range(index.shape[0] // 8)
    ]
    return jnp.concatenate(rows, axis=0)


def flux(psi_up, cond_up, psi_low, cond_low):
    return (cond_up + cond_low) * (
        (psi_up - psi_low) * (0.5 * face_scale / layer_thick) + 0.5 * face_scale
    )


def kernel(
    strips, ks_hbm, al_hbm, th_hbm, p_hbm, t_hbm, a_hbm, rain_hbm, h_hbm, code_hbm, sec_hbm,
    moist, head,
    ks, al, th, pbuf, tbuf, abuf, rain, h0, code, sec, tabs, part, recv1, xs, recv2, c0, c7,
    dn_p, dn_c, up_pc, fb_out, fb_in, fa_out, fa_in,
    E, H, A, colsend, colrecv, heads, rowsend, rowrecv,
    load_sem, misc_sem, s1_send, s1_recv, s2_send, s2_recv,
    face_send, down_recv, up_recv, fb_recv, fa_recv, col_send, col_recv, row_send, row_recv, head_send, head_recv, known,
):
    layers, rows_all, cols_all = pbuf.shape
    chunks, edges = rows_all // R, rows_all // RE
    tile = h0.shape[1]
    wide = tile + LANES
    cols_a = dn_p.shape[1]
    part_a, part_b = pl.ds(0, cols_a), pl.ds(cols_a, cols_all - cols_a)
    body = pl.ds(PAD, rows_all)
    mid, halo = pl.ds(0, tile), pl.ds(tile, LANES)
    last = layers - 1
    depth, strip = lax.axis_index("depth"), lax.axis_index("strips")
    core, chip = depth % 2, depth // 2
    mate = {"depth": chip * 2 + 1 - core}
    cross = {"depth": (depth + 2) % 4}
    above, below = {"depth": depth - 1}, {"depth": depth + 1}
    north, south = {"strips": strip - 1}, {"strips": strip + 1}
    has_up, has_down = depth > 0, depth < 3
    has_north, has_south = strip > 0, strip < strips - 1

    def remote(src, dst, send, recv, device):
        return pltpu.make_async_remote_copy(
            src_ref=src, dst_ref=dst, send_sem=send, recv_sem=recv,
            device_id=device, device_id_type=MESH,
        )

    barrier = pltpu.get_barrier_semaphore()

    def greet(device):
        pl.semaphore_signal(barrier, inc=1, device_id=device, device_id_type=MESH)

    x, y, z, z_count = strip % XS, strip // XS % YS, strip // (XS * YS), strips // (XS * YS)
    start, end = x == 0, x == XS - 1
    corner = start & (y == 0)
    for step in (1, 2, 3):
        greet({"depth": (depth + step) % 4})
    greet({"strips": strip - x + (x + 1) % XS})
    greet({"strips": strip - x + (x + XS - 1) % XS})
    pl.when(start)(lambda: greet({"strips": strip + XS - 2 * XS * y}))
    pl.when(corner & (z > 0))(lambda: greet({"strips": strip - XS * YS}))
    pl.when(corner & (z < z_count - 1))(lambda: greet({"strips": strip + XS * YS}))
    is_start = (XS - x) // XS
    z_sides = (z + z_count - 1) // z_count + (2 * z_count - 2 - z) // z_count
    greeted = 5 + is_start + is_start * (1 - y) * z_sides

    def announce(which, target):
        pl.semaphore_signal(known.at[which], inc=1, device_id={"strips": target}, device_id_type=MESH)

    def announce_first():
        @pl.when(corner)
        def _():
            announce(0, strip + XS - 1)
            announce(0, strip + XS)
            pl.when(z < z_count - 1)(lambda: announce(1, strip + XS))

        pl.when(start & (y == 1) & (z < z_count - 1))(lambda: announce(1, strip - XS))

    def announce_second():
        @pl.when(start & (z < z_count - 1))
        def _():
            pl.semaphore_wait(known.at[1], 1)
            pl.when(y == 0)(lambda: announce(2, strip + XS * YS))
            pl.when(y == 1)(lambda: announce(2, strip + XS - 1))

    def await_announced():
        pl.when((end & (y == 0)) | (start & (y == 1)))(lambda: pl.semaphore_wait(known.at[0], 1))
        pl.when((end & (y == 1) & has_south) | (corner & has_north))(lambda: pl.semaphore_wait(known.at[2], 1))

    def load(which, chunk):
        src, dst = ((p_hbm, pbuf), (t_hbm, tbuf), (a_hbm, abuf))[which]
        where = pl.ds(pl.multiple_of(chunk * R, R), R)
        return pltpu.make_async_copy(src.at[:, where, :], dst.at[:, where, :], load_sem.at[chunk])

    small = [
        pltpu.make_async_copy(src, dst, misc_sem.at[0])
        for i, (src, dst) in enumerate(((h_hbm, h0), (code_hbm, code), (sec_hbm, sec), (rain_hbm, rain)))
    ]
    tables = [
        pltpu.make_async_copy(src, dst, misc_sem.at[1 + i])
        for i, (src, dst) in enumerate(((ks_hbm, ks), (al_hbm, al), (th_hbm, th)))
    ]
    for copy in tables:
        copy.start()
    for i in range(chunks):
        for which in range(3):
            load(which, (i + chunks - 1) % chunks).start()
    for copy in small:
        copy.start()

    for copy in tables:
        copy.wait()
    scales = (1.0, 0.5 * math.log2(math.e), 0.85)
    row = lax.broadcasted_iota(jnp.int32, (8, LANES), 0)
    for i, (ref, scale) in enumerate(zip((ks, al, th), scales)):
        low = high = jnp.zeros((8, LANES), jnp.float32)
        for c in range(ref.shape[0]):
            value = ref[c] * scale
            if c < 8:
                low = jnp.where(row == c, value, low)
            else:
                high = jnp.where(row == c - 8, value, high)
        tabs[i, 0] = low
        tabs[i, 1] = high

    def blank(first, count):
        for q in range(4):
            E[q, first : first + count, :] = jnp.full((count, wide), 1.0 if q == 1 else 0.0, jnp.float32)

    blank(0, PAD - 8)
    blank(PAD + rows_all + 8, PAD - 8)
    pl.when(strip == 0)(lambda: blank(PAD - 8, 8))
    pl.when(strip == strips - 1)(lambda: blank(PAD + rows_all, 8))
    for ref in (A, H):
        for q in range(ref.shape[0]):
            ref[q, 0:PAD, :] = jnp.zeros((PAD, wide), jnp.float32)
            ref[q, PAD + rows_all :, :] = jnp.zeros((PAD, wide), jnp.float32)

    def outside(side):
        group = lax.broadcasted_iota(jnp.int32, (8, LANES), 1) // 8
        for chunk in range(chunks + 1):
            colrecv[side, chunk] = jnp.where(group % 4 == 1, 1.0, 0.0)

    pl.when(depth == 0)(lambda: outside(0))
    pl.when(depth == 3)(lambda: outside(1))

    def order(i):
        return (i + chunks - 1) % chunks

    def stage1(chunk):
        return remote(
            part.at[chunk, 1 - core], recv1.at[chunk], s1_send.at[0], s1_recv.at[chunk], mate
        )

    def stage2(chunk):
        return remote(xs.at[chunk], recv2.at[chunk], s2_send.at[0], s2_recv.at[chunk], cross)

    def column_pass(chunk):
        where = pl.ds(pl.multiple_of(chunk * R, R), R)

        def lane_tile(block, half):
            cols = pl.ds(pl.multiple_of(block * tile + half * LANES, LANES), LANES)
            total = None
            for k in range(layers):
                p, t, a = pbuf[k, where, cols], tbuf[k, where, cols], abuf[k, where, cols]
                index, upper = t & 7, t >= 8
                sat, shape, pore = (
                    jnp.where(upper, pick(tabs[i, 1], index), pick(tabs[i, 0], index)) for i in range(3)
                )
                wet = jnp.exp2(shape * jnp.minimum(p, 0.0))
                cond = sat * (wet * wet) * a.astype(jnp.float32)
                dry = pore * (1.0 - wet)
                water = pore * (1.0 / 0.85) - dry
                charge = cond * wet
                if k == 0:
                    c0[where, cols] = cond
                    total = (cond, dry, charge)
                else:
                    total = (total[0] + cond, total[1] + dry, total[2] + charge)
                    inner = flux(p_up, cond_up, p, cond)
                    moist[k - 1, where, cols] = water_up - inner
                    water = water + inner
                p_up, cond_up, water_up = p, cond, water
            moist[last, where, cols] = water_up
            c7[where, cols] = cond_up
            for q in range(3):
                part[chunk, block % 2, block // 2, q, :, half * LANES : (half + 1) * LANES] = total[q]

        @pl.loop(0, cols_all // tile)
        def _(block):
            for half in range(tile // LANES):
                lane_tile(block, half)

    half = rows_all // 2

    def down_p(e):
        where = pl.ds(pl.multiple_of(e * RE, RE), RE)
        k = e // (edges // 2)
        return remote(pbuf.at[last, where, part_a], dn_p.at[where], face_send.at[0], down_recv.at[2 + k], below)

    def down_c(k):
        where = pl.ds(k * half, half)
        return remote(c7.at[where, part_a], dn_c.at[where], face_send.at[1], down_recv.at[k], below)

    def up_message(which, e):
        where = pl.ds(pl.multiple_of(e * RE, RE), RE)
        src = (pbuf.at[0, where, part_b], c0.at[where, part_b])[which]
        return remote(src, up_pc.at[e, which], face_send.at[2 + which], up_recv.at[e], above)

    def flux_down(e):
        where = pl.ds(pl.multiple_of(e * RE, RE), RE)
        return remote(fb_out.at[where], fb_in.at[where], face_send.at[4], fb_recv.at[0], below)

    def flux_up(e):
        where = pl.ds(pl.multiple_of(e * RE, RE), RE)
        return remote(fa_out.at[where], fa_in.at[where], face_send.at[5], fa_recv.at[0], above)

    def finish(chunk):
        stage2(chunk).wait_recv()
        here = pl.ds(pl.multiple_of(chunk * R, R), R)
        there = pl.ds(pl.multiple_of(PAD + chunk * R, 8), R)
        trans, store, charge = (
            (part[chunk, core, chip, q] + recv1[chunk, chip, q]) + recv2[chunk, q] for q in range(3)
        )
        store = spec_yield + store * layer_thick
        kind = code[here, :]
        river = jnp.where(kind == 1, river_cond, jnp.where(kind == 2, fixed_cond, 0.0))
        old = h0[here, :]
        root = jnp.sqrt(trans * layer_thick)
        E[0, there, mid] = root
        E[1, there, mid] = store + river
        E[2, there, mid] = store * old + charge * (leak_rate * layer_thick) + river * sec[here, :]
        E[3, there, mid] = root * old
        pack(chunk, tiles_of(chunk))

    lane = lax.broadcasted_iota(jnp.int32, (8, LANES), 1) // 8

    def column_halo(side, chunk):
        return remote(
            colsend.at[side, chunk], colrecv.at[side, chunk],
            col_send.at[side], col_recv.at[chunk], (below, above)[side],
        )

    def pack_tiles(side, chunk, tiles):
        edge = pl.ds(tile - LANES if side == 0 else 0, LANES)
        out = jnp.zeros((8, LANES), jnp.float32)
        for q in range(4):
            for h in range(2):
                group = q + 4 * h
                shift = (8 * group + (8 if side == 0 else 0)) % LANES
                value = E[q, tiles[h], edge]
                out = jnp.where(lane == group, pltpu.roll(value, shift, 1) if shift else value, out)
        colsend[side, chunk] = out
        column_halo(side, chunk).start()

    def tiles_of(chunk):
        return [pl.ds(pl.multiple_of(PAD + chunk * R + 8 * h, 8), 8) for h in range(2)]

    halo_tiles = [pl.ds(PAD - 8, 8), pl.ds(PAD + rows_all, 8)]

    def pack(chunk, tiles):
        pl.when(has_down)(lambda: pack_tiles(0, chunk, tiles))
        pl.when(has_up)(lambda: pack_tiles(1, chunk, tiles))

    def unpack(chunk, tiles=None):
        pl.when(depth == 0)(lambda: column_halo(1, chunk).wait_recv())
        pl.when(depth == 3)(lambda: column_halo(0, chunk).wait_recv())

        @pl.when(has_up & has_down)
        def _():
            remote(
                colsend.at[:, chunk], colrecv.at[:, chunk], col_send.at[0], col_recv.at[chunk], below
            ).wait_recv()

        west, east = colrecv[0, chunk], colrecv[1, chunk]
        for q in range(4):
            for h in range(2):
                group = q + 4 * h
                moved = pltpu.roll(west, 120 - 8 * group, 1)
                E[q, (tiles or tiles_of(chunk))[h], halo] = jnp.where(
                    lane < 8, pltpu.roll(east, LANES - 8 * group, 1) if group else east, moved
                )

    row8 = lax.broadcasted_iota(jnp.int32, (8, LANES), 0)
    turns = ((0, 3, 6, 0, 2), (3, 6, 0, 2, 4))

    def turned(value, shift):
        return pltpu.roll(value, shift % 8, 0) if shift % 8 else value

    def row_halo(side):
        return remote(rowsend.at[side], rowrecv.at[side], row_send.at[side], row_recv.at[side], (north, south)[side])

    def send_rows(side):
        mine = pl.ds(PAD if side == 0 else PAD + rows_all - 8, 8)
        for k in range(2):
            cols = pl.ds(k * LANES, LANES)
            root, product, base = (turned(E[q, mine, cols], turns[side][n]) for n, q in enumerate((0, 3, 1)))
            rowsend[side, :, cols] = jnp.where(row8 < 3, root, jnp.where(row8 < 6, product, base))
        first, second = (turned(E[2, mine, pl.ds(k * LANES, LANES)], turns[side][3 + k]) for k in range(2))
        rowsend[side, :, 2 * LANES :] = jnp.where(row8 < 2, first, second)
        row_halo(side).start()

    def take_rows(side):
        row_halo(side).wait_recv()
        theirs = pl.ds(PAD + rows_all if side == 0 else PAD - 8, 8)
        for k in range(2):
            cols = pl.ds(k * LANES, LANES)
            value = rowrecv[side, :, cols]
            for n, q in enumerate((0, 3, 1)):
                E[q, theirs, cols] = turned(value, 8 - turns[side][n])
            E[2, theirs, cols] = turned(rowrecv[side, :, 2 * LANES :], 8 - turns[side][3 + k])

    def send_pressures(e):
        pl.when(has_down)(lambda: down_p(e).start())
        pl.when(has_up)(lambda: up_message(0, e).start())

    @pl.loop(0, chunks + 2)
    def _(i):
        @pl.when(i < chunks)
        def _():
            three = pl.ds(0, 3 * R)
            pltpu.make_async_copy(p_hbm.at[:, three, :], pbuf.at[:, three, :], load_sem.at[order(i)]).wait()

        @pl.when((i == 0) & (x > 0))
        def _():
            pl.semaphore_wait(barrier, greeted)
            announce_first()

        @pl.when((i < EARLY) & (i + x > 0))
        def _():
            send_pressures(order(i))

        @pl.when(i < chunks)
        def _():
            column_pass(order(i))

        @pl.when((i == 0) & start)
        def _():
            pl.semaphore_wait(barrier, greeted)
            announce_first()
            send_pressures(order(i))

        pl.when(i == chunks // 2)(announce_second)

        @pl.when(i == chunks)
        def _():
            seven = pl.ds(0, 3 + cols_all // tile)
            pltpu.make_async_copy(p_hbm.at[seven, :, mid], pbuf.at[seven, :, mid], misc_sem.at[0]).wait()

        @pl.when(i >= chunks)
        def _():
            finish(order(i - chunks))

        @pl.when(i > 1)
        def _():
            chunk = order(i - 2)
            stage1(chunk).wait_recv()
            xs[chunk] = part[chunk, core, 1 - chip] + recv1[chunk, 1 - chip]

        @pl.when(i < chunks)
        def _():
            stage1(order(i)).start()

        @pl.when(i > 1)
        def _():
            stage2(order(i - 2)).start()

    def post_faces(first, last_one):
        @pl.loop(first, last_one)
        def _(e):
            @pl.when(has_up)
            def _():
                pl.when((e >= EARLY - 1) & (e < edges - 1))(lambda: up_message(0, e).start())
                up_message(1, e).start()

    @pl.when(depth == 0)
    def _():
        moist[0] = moist[0] + face_scale * rain[...]

    def face_step(e):
        where = pl.ds(pl.multiple_of(e * RE, RE), RE)

        @pl.when(has_down)
        def _():
            remote(up_pc.at[e], up_pc.at[e], face_send.at[2], up_recv.at[e], below).wait_recv()
            value = flux(pbuf[last, where, part_b], c7[where, part_b], up_pc[e, 0], up_pc[e, 1])
            fb_out[where] = value
            moist[last, where, part_b] = moist[last, where, part_b] - value
            flux_down(e).start()

        @pl.when(has_up)
        def _():
            for k in range(2):

                @pl.when(e == k * (edges // 2))
                def _():
                    where = pl.ds(k * half, half)
                    remote(dn_p.at[where], dn_p.at[where], face_send.at[0], down_recv.at[2 + k], above).wait_recv()
                    down_c(k).wait_recv()

            value = flux(dn_p[where], dn_c[where], pbuf[0, where, part_a], c0[where, part_a])
            fa_out[where] = value
            moist[0, where, part_a] = moist[0, where, part_a] + value
            flux_up(e).start()

    sub = lax.broadcasted_iota(jnp.int32, (8, wide), 0)

    def rows_of(t, count=1):
        return pl.ds(pl.multiple_of(8 * t, 8), 8 * count)

    def around(ref, q, t):
        north_t, a, b, south_t = (ref[q, rows_of(t + k), :] for k in (-1, 0, 1, 2))

        def sums(before, here, after):
            down = [pltpu.roll(v, 1, 0) for v in (before, here)]
            up = [pltpu.roll(v, 7, 0) for v in (here, after)]
            return (
                pltpu.roll(here, 1, 1)
                + pltpu.roll(here, wide - 1, 1)
                + jnp.where(sub == 0, down[0], down[1])
                + jnp.where(sub == 7, up[1], up[0])
            )

        return jnp.concatenate([sums(north_t, a, b), sums(a, b, south_t)], axis=0)

    def wave(j, stages):
        at = (2 * j + 2, 2 * j, 2 * j - 3, 2 * j - 6)
        out = []
        if 3 in stages:
            here = rows_of(at[3], 2)
            out.append((H, 2, here, A[2, here, :] + A[3, here, :] * around(H, 1, at[3])))
        if 2 in stages:
            here = rows_of(at[2], 2)
            out.append((H, 1, here, A[0, here, :] + A[1, here, :] * around(H, 0, at[2])))
        if 1 in stages:
            here = rows_of(at[1], 2)
            out.append((H, 0, here, A[0, here, :] + A[1, here, :] * around(E, 3, at[1])))
        if 0 in stages:
            here = rows_of(at[0], 2)
            root = E[0, here, :]
            scale = 1.0 / (E[1, here, :] + root * around(E, 0, at[0]))
            free, bound = E[2, here, :] * scale, root * scale
            out += [(A, 0, here, root * free), (A, 1, here, root * bound), (A, 2, here, free), (A, 3, here, bound)]
        for ref, q, here, value in out:
            ref[q, here, :] = value

    def head_copy(chunk, source):
        where = pl.ds(pl.multiple_of(chunk * R, R), R)
        return remote(
            heads.at[source, where], heads.at[source, where],
            head_send.at[0], head_recv.at[source], {"depth": 3},
        )

    def hand_on(chunk):
        where = pl.ds(pl.multiple_of(chunk * R, R), R)
        value = H[SWEEPS - 1, pl.ds(pl.multiple_of(PAD + chunk * R, 8), R), mid]
        heads[depth, where] = value
        head[where, :] = value
        pl.when(depth < 3)(lambda: head_copy(chunk, depth).start())

    await_announced()
    pl.when(has_north)(lambda: send_rows(0))
    pl.when(has_south)(lambda: send_rows(1))

    def posts(down, up):
        for copy in down:
            pl.when(has_down)(copy)
        post_faces(*up)

    finish(1)
    finish(2)
    finish(3)
    posts([lambda: down_c(0).start()], (0, 2))
    finish(4)
    posts([lambda: down_p(EARLY - 1).start()], (2, 3))
    finish(5)
    posts([lambda: down_c(1).start()], (3, 4))
    finish(6)

    pl.when(has_south)(lambda: take_rows(0))
    pl.when(has_north)(lambda: take_rows(1))
    pack(chunks, halo_tiles)
    posts([lambda e=e: down_p(e).start() for e in range(EARLY, edges - 1)], (4, edges))
    face_step(0)
    face_step(1)

    @pl.loop(0, chunks - 3)
    def _(chunk):
        unpack(chunk)

    unpack(chunks - 1)
    face_step(2)
    unpack(chunks, halo_tiles)

    every = (0, 1, 2, 3)
    wave(0, (0,))
    wave(1, (0, 1))
    wave(2, (0, 1, 2))
    wave(3, (0, 1, 2))
    wave(4, (0, 1, 2, 3))
    face_step(3)

    @pl.loop(5, chunks - 1)
    def _(j):
        unpack(j)
        wave(j, every)
        hand_on(j - 5)

    face_step(4)

    @pl.loop(chunks - 1, chunks + 1)
    def _(j):
        wave(j, every)
        hand_on(j - 5)

    for j, stages in ((chunks + 1, (1, 2, 3)), (chunks + 2, (2, 3)), (chunks + 3, (2, 3)), (chunks + 4, (3,))):
        wave(j, stages)
        hand_on(j - 5)

    @pl.loop(5, edges)
    def _(e):
        face_step(e)

    @pl.when(depth == 3)
    def _():
        for block in range(4):
            if block < 3:
                remote(heads.at[block], heads.at[block], head_send.at[0], head_recv.at[block], {"depth": 0}).wait_recv()
            cols = pl.ds(block * tile, tile)
            bottom = c7[:, cols] * (
                (pbuf[last, :, cols] - heads[block]) * (2.0 * face_scale / layer_thick) + face_scale
            )
            moist[last, :, cols] = moist[last, :, cols] - bottom

    @pl.when(has_down)
    def _():
        remote(fa_in, fa_in, face_send.at[5], fa_recv.at[0], below).wait_recv()
        moist[last, :, part_a] = moist[last, :, part_a] - fa_in[...]

    @pl.when(has_up)
    def _():
        remote(fb_in, fb_in, face_send.at[4], fb_recv.at[0], above).wait_recv()
        moist[0, :, part_b] = moist[0, :, part_b] + fb_in[...]

    remote(part.at[:, 1 - core], recv1, s1_send.at[0], s1_recv.at[0], mate).wait_send()
    remote(xs, recv2, s2_send.at[0], s2_recv.at[0], cross).wait_send()

    @pl.when(has_down)
    def _():
        remote(c7.at[:, part_a], dn_p, face_send.at[0], down_recv.at[2], below).wait_send()
        remote(c7.at[:, part_a], dn_c, face_send.at[1], down_recv.at[1], below).wait_send()
        remote(fb_out, fb_in, face_send.at[4], fb_recv.at[0], below).wait_send()
        remote(colsend.at[0], colrecv.at[0], col_send.at[0], col_recv.at[0], below).wait_send()
        remote(heads.at[depth], heads.at[depth], head_send.at[0], head_recv.at[depth], {"depth": 3}).wait_send()

    @pl.when(has_up)
    def _():
        remote(c0.at[:, part_b], fb_in, face_send.at[2], up_recv.at[0], above).wait_send()
        remote(c0.at[:, part_b], fb_in, face_send.at[3], up_recv.at[0], above).wait_send()
        remote(fa_out, fa_in, face_send.at[5], fa_recv.at[0], above).wait_send()
        remote(colsend.at[1], colrecv.at[1], col_send.at[1], col_recv.at[0], above).wait_send()

    pl.when(has_north)(lambda: row_halo(0).wait_send())
    pl.when(has_south)(lambda: row_halo(1).wait_send())


def store_kernel(moist, head, moist_out, head_out, sems):
    copies = [pltpu.make_async_copy(head, head_out, sems.at[0])]
    for k in range(moist.shape[0]):
        copies.append(pltpu.make_async_copy(moist.at[k], moist_out.at[k], sems.at[k + 1]))
    for copy in copies:
        copy.start()
    for copy in copies:
        copy.wait()


def shards(strips, pressure, texture, active, rain, k_sat, alpha, theta_sat, head_old, cell_code, section):
    layers, rows, cols = pressure.shape
    tile = head_old.shape[1]
    wide = tile + LANES
    cols_a = 3 * LANES
    cols_b = cols - cols_a
    chunks, edges = rows // R, rows // RE
    f32 = jnp.float32
    vmem = lambda *shape: pltpu.VMEM(shape, f32)
    dma = lambda *shape: pltpu.SemaphoreType.DMA(shape)
    table = pltpu.SMEM(k_sat.shape, f32)
    scratch = [
        table,
        table,
        table,
        vmem(layers, rows, cols),
        pltpu.VMEM((layers, rows, cols), jnp.int32),
        pltpu.VMEM((layers, rows, cols), jnp.int32),
        vmem(rows, cols),
        vmem(rows, tile),
        pltpu.VMEM((rows, tile), jnp.int32),
        vmem(rows, tile),
        vmem(3, 2, 8, LANES),
        vmem(chunks, 2, 2, 3, R, tile),
        vmem(chunks, 2, 3, R, tile),
        vmem(chunks, 3, R, tile),
        vmem(chunks, 3, R, tile),
        vmem(rows, cols),
        vmem(rows, cols),
        vmem(rows, cols_a),
        vmem(rows, cols_a),
        vmem(edges, 2, RE, cols_b),
        vmem(rows, cols_b),
        vmem(rows, cols_b),
        vmem(rows, cols_a),
        vmem(rows, cols_a),
        vmem(4, rows + 2 * PAD, wide),
        vmem(SWEEPS, rows + 2 * PAD, wide),
        vmem(4, rows + 2 * PAD, wide),
        vmem(2, chunks + 1, 8, LANES),
        vmem(2, chunks + 1, 8, LANES),
        vmem(4, rows, tile),
        vmem(2, 8, 3 * LANES),
        vmem(2, 8, 3 * LANES),
        dma(chunks),
        dma(4),
        dma(1),
        dma(chunks),
        dma(1),
        dma(chunks),
        dma(6),
        dma(4),
        dma(edges),
        dma(1),
        dma(1),
        dma(2),
        dma(chunks + 1),
        dma(2),
        dma(2),
        dma(1),
        dma(4),
        pltpu.SemaphoreType.REGULAR((3,)),
    ]
    anywhere = pl.BlockSpec(memory_space=pltpu.HBM)
    moist, head = pl.pallas_call(
        functools.partial(kernel, strips),
        out_shape=(
            pltpu.VMEM((layers, rows, cols), f32),
            pltpu.VMEM((rows, tile), f32),
        ),
        in_specs=[anywhere] * 10,
        out_specs=(pl.BlockSpec(memory_space=pltpu.VMEM), pl.BlockSpec(memory_space=pltpu.VMEM)),
        scratch_shapes=scratch,
        compiler_params=pltpu.CompilerParams(
            collective_id=0, has_side_effects=True, vmem_limit_bytes=59 * 2**20
        ),
        name="soil_column",
    )(k_sat, alpha, theta_sat, pressure, texture, active, rain, head_old, cell_code, section)
    on_chip = pl.BlockSpec(memory_space=pltpu.VMEM)
    return pl.pallas_call(
        store_kernel,
        out_shape=(
            jax.ShapeDtypeStruct((layers, rows, cols), f32),
            jax.ShapeDtypeStruct((rows, tile), f32),
        ),
        in_specs=[on_chip] * 2,
        out_specs=(anywhere, anywhere),
        scratch_shapes=[dma(layers + 1)],
        compiler_params=pltpu.CompilerParams(vmem_limit_bytes=2**20),
        name="store",
    )(pltpu.with_memory_space_constraint(moist, pltpu.VMEM), pltpu.with_memory_space_constraint(head, pltpu.VMEM))


def solution(mesh):
    in_specs = (
        P("depth", "strips", None),
        P("depth", "strips", None),
        P("depth", "strips", None),
        P("strips", None),
        P(),
        P(),
        P(),
        P("strips", "depth"),
        P("strips", "depth"),
        P("strips", "depth"),
    )
    out_specs = (P("depth", "strips", None), P("strips", "depth"))
    body = functools.partial(shards, mesh.shape["strips"])
    return jax.shard_map(body, mesh=mesh, in_specs=in_specs, out_specs=out_specs, check_vma=False)
```

```python
import functools
import math

import jax
import jax.numpy as jnp
from jax import lax
from jax.experimental import pallas as pl
from jax.experimental.pallas import tpu as pltpu
from jax.sharding import PartitionSpec as P

MESH = pl.DeviceIdType.MESH
SWEEPS = 3

layer_thick = 0.05
soil_step = 0.0002
spec_yield = 0.02
leak_rate = 0.5
river_cond = 0.5
fixed_cond = 3.0
face_scale = soil_step / layer_thick

R = 16
RE = R
EARLY = 4
XS, YS = 4, 2
PAD = 24
LANES = 128


def pick(table, index):
    dims = lax.GatherDimensionNumbers(
        offset_dims=(),
        collapsed_slice_dims=(0,),
        start_index_map=(0,),
        operand_batching_dims=(1,),
        start_indices_batching_dims=(1,),
    )
    rows = [
        lax.gather(
            table,
            index[8 * i : 8 * i + 8, :, None],
            dims,
            slice_sizes=(1, 1),
            mode=lax.GatherScatterMode.PROMISE_IN_BOUNDS,
        )
        for i in range(index.shape[0] // 8)
    ]
    return jnp.concatenate(rows, axis=0)


def flux(psi_up, cond_up, psi_low, cond_low):
    return (cond_up + cond_low) * (
        (psi_up - psi_low) * (0.5 * face_scale / layer_thick) + 0.5 * face_scale
    )


def kernel(
    strips, ks_hbm, al_hbm, th_hbm, p_hbm, t_hbm, a_hbm, rain_hbm, h_hbm, code_hbm, sec_hbm,
    moist, head,
    ks, al, th, pbuf, tbuf, abuf, rain, h0, code, sec, tabs, part, recv1, xs, recv2, c0, c7,
    dn_p, dn_c, up_pc, fb_out, fb_in, fa_out, fa_in,
    E, H, A, colsend, colrecv, heads, rowsend, rowrecv,
    load_sem, misc_sem, s1_send, s1_recv, s2_send, s2_recv,
    face_send, down_recv, up_recv, fb_recv, fa_recv, col_send, col_recv, row_send, row_recv, head_send, head_recv, known,
):
    layers, rows_all, cols_all = pbuf.shape
    chunks, edges = rows_all // R, rows_all // RE
    tile = h0.shape[1]
    wide = tile + LANES
    cols_a = dn_p.shape[1]
    part_a, part_b = pl.ds(0, cols_a), pl.ds(cols_a, cols_all - cols_a)
    body = pl.ds(PAD, rows_all)
    mid, halo = pl.ds(0, tile), pl.ds(tile, LANES)
    last = layers - 1
    depth, strip = lax.axis_index("depth"), lax.axis_index("strips")
    core, chip = depth % 2, depth // 2
    mate = {"depth": chip * 2 + 1 - core}
    cross = {"depth": (depth + 2) % 4}
    above, below = {"depth": depth - 1}, {"depth": depth + 1}
    north, south = {"strips": strip - 1}, {"strips": strip + 1}
    has_up, has_down = depth > 0, depth < 3
    has_north, has_south = strip > 0, strip < strips - 1

    def remote(src, dst, send, recv, device):
        return pltpu.make_async_remote_copy(
            src_ref=src, dst_ref=dst, send_sem=send, recv_sem=recv,
            device_id=device, device_id_type=MESH,
        )

    barrier = pltpu.get_barrier_semaphore()

    def greet(device):
        pl.semaphore_signal(barrier, inc=1, device_id=device, device_id_type=MESH)

    x, y, z, z_count = strip % XS, strip // XS % YS, strip // (XS * YS), strips // (XS * YS)
    start, end = x == 0, x == XS - 1
    corner = start & (y == 0)
    for step in (1, 2, 3):
        greet({"depth": (depth + step) % 4})
    greet({"strips": strip - x + (x + 1) % XS})
    greet({"strips": strip - x + (x + XS - 1) % XS})
    pl.when(start)(lambda: greet({"strips": strip + XS - 2 * XS * y}))
    pl.when(corner & (z > 0))(lambda: greet({"strips": strip - XS * YS}))
    pl.when(corner & (z < z_count - 1))(lambda: greet({"strips": strip + XS * YS}))
    is_start = (XS - x) // XS
    z_sides = (z + z_count - 1) // z_count + (2 * z_count - 2 - z) // z_count
    greeted = 5 + is_start + is_start * (1 - y) * z_sides

    def announce(which, target):
        pl.semaphore_signal(known.at[which], inc=1, device_id={"strips": target}, device_id_type=MESH)

    def announce_first():
        @pl.when(corner)
        def _():
            announce(0, strip + XS - 1)
            announce(0, strip + XS)
            pl.when(z < z_count - 1)(lambda: announce(1, strip + XS))

        pl.when(start & (y == 1) & (z < z_count - 1))(lambda: announce(1, strip - XS))

    def announce_second():
        @pl.when(start & (z < z_count - 1))
        def _():
            pl.semaphore_wait(known.at[1], 1)
            pl.when(y == 0)(lambda: announce(2, strip + XS * YS))
            pl.when(y == 1)(lambda: announce(2, strip + XS - 1))

    def await_announced():
        pl.when((end & (y == 0)) | (start & (y == 1)))(lambda: pl.semaphore_wait(known.at[0], 1))
        pl.when((end & (y == 1) & has_south) | (corner & has_north))(lambda: pl.semaphore_wait(known.at[2], 1))

    def load(which, chunk):
        src, dst = ((p_hbm, pbuf), (t_hbm, tbuf), (a_hbm, abuf))[which]
        where = pl.ds(pl.multiple_of(chunk * R, R), R)
        return pltpu.make_async_copy(src.at[:, where, :], dst.at[:, where, :], load_sem.at[chunk])

    small = [
        pltpu.make_async_copy(src, dst, misc_sem.at[0])
        for i, (src, dst) in enumerate(((h_hbm, h0), (code_hbm, code), (sec_hbm, sec), (rain_hbm, rain)))
    ]
    tables = [
        pltpu.make_async_copy(src, dst, misc_sem.at[1 + i])
        for i, (src, dst) in enumerate(((ks_hbm, ks), (al_hbm, al), (th_hbm, th)))
    ]
    for copy in tables:
        copy.start()
    for i in range(chunks):
        for which in range(3):
            load(which, (i + chunks - 1) % chunks).start()
    for copy in small:
        copy.start()

    for copy in tables:
        copy.wait()
    scales = (1.0, 0.5 * math.log2(math.e), 0.85)
    row = lax.broadcasted_iota(jnp.int32, (8, LANES), 0)
    for i, (ref, scale) in enumerate(zip((ks, al, th), scales)):
        low = high = jnp.zeros((8, LANES), jnp.float32)
        for c in range(ref.shape[0]):
            value = ref[c] * scale
            if c < 8:
                low = jnp.where(row == c, value, low)
            else:
                high = jnp.where(row == c - 8, value, high)
        tabs[i, 0] = low
        tabs[i, 1] = high

    def blank(first, count):
        for q in range(4):
            E[q, first : first + count, :] = jnp.full((count, wide), 1.0 if q == 1 else 0.0, jnp.float32)

    blank(0, PAD - 8)
    blank(PAD + rows_all + 8, PAD - 8)
    pl.when(strip == 0)(lambda: blank(PAD - 8, 8))
    pl.when(strip == strips - 1)(lambda: blank(PAD + rows_all, 8))
    for ref in (A, H):
        for q in range(ref.shape[0]):
            ref[q, 0:PAD, :] = jnp.zeros((PAD, wide), jnp.float32)
            ref[q, PAD + rows_all :, :] = jnp.zeros((PAD, wide), jnp.float32)

    def outside(side):
        group = lax.broadcasted_iota(jnp.int32, (8, LANES), 1) // 8
        for chunk in range(colrecv.shape[1]):
            colrecv[side, chunk] = jnp.where(group % 4 == 1, 1.0, 0.0)

    pl.when(depth == 0)(lambda: outside(0))
    pl.when(depth == 3)(lambda: outside(1))

    def order(i):
        return (i + chunks - 1) % chunks

    def stage1(chunk):
        return remote(
            part.at[chunk, 1 - core], recv1.at[chunk], s1_send.at[0], s1_recv.at[chunk], mate
        )

    def stage2(chunk):
        return remote(xs.at[chunk], recv2.at[chunk], s2_send.at[0], s2_recv.at[chunk], cross)

    def column_pass(chunk):
        where = pl.ds(pl.multiple_of(chunk * R, R), R)

        def lane_tile(block, half):
            cols = pl.ds(pl.multiple_of(block * tile + half * LANES, LANES), LANES)
            total = None
            for k in range(layers):
                p, t, a = pbuf[k, where, cols], tbuf[k, where, cols], abuf[k, where, cols]
                index, upper = t & 7, t >= 8
                sat, shape, pore = (
                    jnp.where(upper, pick(tabs[i, 1], index), pick(tabs[i, 0], index)) for i in range(3)
                )
                wet = jnp.exp2(shape * jnp.minimum(p, 0.0))
                cond = sat * (wet * wet) * a.astype(jnp.float32)
                dry = pore * (1.0 - wet)
                water = pore * (1.0 / 0.85) - dry
                charge = cond * wet
                if k == 0:
                    c0[where, cols] = cond
                    total = (cond, dry, charge)
                else:
                    total = (total[0] + cond, total[1] + dry, total[2] + charge)
                    inner = flux(p_up, cond_up, p, cond)
                    moist[k - 1, where, cols] = water_up - inner
                    water = water + inner
                p_up, cond_up, water_up = p, cond, water
            moist[last, where, cols] = water_up
            c7[where, cols] = cond_up
            for q in range(3):
                part[chunk, block % 2, block // 2, q, :, half * LANES : (half + 1) * LANES] = total[q]

        @pl.loop(0, cols_all // tile)
        def _(block):
            for half in range(tile // LANES):
                lane_tile(block, half)

    half = rows_all // 2

    def down_p(e):
        where = pl.ds(pl.multiple_of(e * RE, RE), RE)
        k = e // (edges // 2)
        return remote(pbuf.at[last, where, part_a], dn_p.at[where], face_send.at[0], down_recv.at[2 + k], below)

    def down_c(k):
        where = pl.ds(k * half, half)
        return remote(c7.at[where, part_a], dn_c.at[where], face_send.at[1], down_recv.at[k], below)

    def up_message(which, e):
        where = pl.ds(pl.multiple_of(e * RE, RE), RE)
        src = (pbuf.at[0, where, part_b], c0.at[where, part_b])[which]
        return remote(src, up_pc.at[e, which], face_send.at[2 + which], up_recv.at[e], above)

    def flux_down(e):
        where = pl.ds(pl.multiple_of(e * RE, RE), RE)
        return remote(fb_out.at[where], fb_in.at[where], face_send.at[4], fb_recv.at[0], below)

    def flux_up(e):
        where = pl.ds(pl.multiple_of(e * RE, RE), RE)
        return remote(fa_out.at[where], fa_in.at[where], face_send.at[5], fa_recv.at[0], above)

    def finish(chunk):
        stage2(chunk).wait_recv()
        here = pl.ds(pl.multiple_of(chunk * R, R), R)
        there = pl.ds(pl.multiple_of(PAD + chunk * R, 8), R)
        trans, store, charge = (
            (part[chunk, core, chip, q] + recv1[chunk, chip, q]) + recv2[chunk, q] for q in range(3)
        )
        store = spec_yield + store * layer_thick
        kind = code[here, :]
        river = jnp.where(kind == 1, river_cond, jnp.where(kind == 2, fixed_cond, 0.0))
        old = h0[here, :]
        root = jnp.sqrt(trans * layer_thick)
        E[0, there, mid] = root
        E[1, there, mid] = store + river
        E[2, there, mid] = store * old + charge * (leak_rate * layer_thick) + river * sec[here, :]
        E[3, there, mid] = root * old

    lane = lax.broadcasted_iota(jnp.int32, (8, LANES), 1) // 8

    def column_halo(side, chunk):
        return remote(
            colsend.at[side, chunk], colrecv.at[side, chunk],
            col_send.at[side], col_recv.at[chunk], (below, above)[side],
        )

    def pack_tiles(side, chunk, tiles):
        edge = pl.ds(tile - LANES if side == 0 else 0, LANES)
        out = jnp.zeros((8, LANES), jnp.float32)
        for q in range(4):
            for h in range(len(tiles)):
                group = q + 4 * h
                shift = (8 * group + (8 if side == 0 else 0)) % LANES
                value = E[q, tiles[h], edge]
                out = jnp.where(lane == group, pltpu.roll(value, shift, 1) if shift else value, out)
        colsend[side, chunk] = out
        column_halo(side, chunk).start()

    def tiles_of(chunk):
        return [pl.ds(pl.multiple_of(PAD + chunk * R + 8 * h, 8), 8) for h in range(2)]

    halo_tiles = [pl.ds(PAD - 8, 8), pl.ds(PAD + rows_all, 8)]
    pairs = [tiles_of(chunks - 1) + tiles_of(0), tiles_of(1) + tiles_of(2), tiles_of(3) + tiles_of(4)]
    pairs += [tiles_of(5), tiles_of(6) + halo_tiles]

    def pack(m):
        pl.when(has_down)(lambda: pack_tiles(0, m, pairs[m]))
        pl.when(has_up)(lambda: pack_tiles(1, m, pairs[m]))

    def unpack(chunk):
        pl.when(depth == 0)(lambda: column_halo(1, chunk).wait_recv())
        pl.when(depth == 3)(lambda: column_halo(0, chunk).wait_recv())

        @pl.when(has_up & has_down)
        def _():
            remote(
                colsend.at[:, chunk], colrecv.at[:, chunk], col_send.at[0], col_recv.at[chunk], below
            ).wait_recv()

        west, east = colrecv[0, chunk], colrecv[1, chunk]
        for q in range(4):
            for h, there in enumerate(pairs[chunk]):
                group = q + 4 * h
                moved = pltpu.roll(west, 120 - 8 * group, 1)
                E[q, there, halo] = jnp.where(
                    lane < 8, pltpu.roll(east, LANES - 8 * group, 1) if group else east, moved
                )

    row8 = lax.broadcasted_iota(jnp.int32, (8, LANES), 0)
    turns = ((0, 3, 6, 0, 2), (3, 6, 0, 2, 4))

    def turned(value, shift):
        return pltpu.roll(value, shift % 8, 0) if shift % 8 else value

    def row_halo(side):
        return remote(rowsend.at[side], rowrecv.at[side], row_send.at[side], row_recv.at[side], (north, south)[side])

    def send_rows(side):
        mine = pl.ds(PAD if side == 0 else PAD + rows_all - 8, 8)
        for k in range(2):
            cols = pl.ds(k * LANES, LANES)
            root, product, base = (turned(E[q, mine, cols], turns[side][n]) for n, q in enumerate((0, 3, 1)))
            rowsend[side, :, cols] = jnp.where(row8 < 3, root, jnp.where(row8 < 6, product, base))
        first, second = (turned(E[2, mine, pl.ds(k * LANES, LANES)], turns[side][3 + k]) for k in range(2))
        rowsend[side, :, 2 * LANES :] = jnp.where(row8 < 2, first, second)
        row_halo(side).start()

    def take_rows(side):
        row_halo(side).wait_recv()
        theirs = pl.ds(PAD + rows_all if side == 0 else PAD - 8, 8)
        for k in range(2):
            cols = pl.ds(k * LANES, LANES)
            value = rowrecv[side, :, cols]
            for n, q in enumerate((0, 3, 1)):
                E[q, theirs, cols] = turned(value, 8 - turns[side][n])
            E[2, theirs, cols] = turned(rowrecv[side, :, 2 * LANES :], 8 - turns[side][3 + k])

    def send_pressures(e):
        pl.when(has_down)(lambda: down_p(e).start())
        pl.when(has_up)(lambda: up_message(0, e).start())

    @pl.loop(0, chunks + 2)
    def _(i):
        @pl.when(i < chunks)
        def _():
            three = pl.ds(0, 3 * R)
            pltpu.make_async_copy(p_hbm.at[:, three, :], pbuf.at[:, three, :], load_sem.at[order(i)]).wait()

        @pl.when((i == 0) & (x > 0))
        def _():
            pl.semaphore_wait(barrier, greeted)
            announce_first()

        @pl.when((i < EARLY) & (i + x > 0))
        def _():
            send_pressures(order(i))

        @pl.when(i < chunks)
        def _():
            column_pass(order(i))

        @pl.when((i == 0) & start)
        def _():
            pl.semaphore_wait(barrier, greeted)
            announce_first()
            send_pressures(order(i))

        pl.when(i == chunks // 2)(announce_second)

        @pl.when(i == chunks)
        def _():
            seven = pl.ds(0, 3 + cols_all // tile)
            pltpu.make_async_copy(p_hbm.at[seven, :, mid], pbuf.at[seven, :, mid], misc_sem.at[0]).wait()

        @pl.when(i >= chunks)
        def _():
            finish(order(i - chunks))

        @pl.when(i > 1)
        def _():
            chunk = order(i - 2)
            stage1(chunk).wait_recv()
            xs[chunk] = part[chunk, core, 1 - chip] + recv1[chunk, 1 - chip]

        @pl.when(i < chunks)
        def _():
            stage1(order(i)).start()

        @pl.when(i > 1)
        def _():
            stage2(order(i - 2)).start()

    def post_faces(first, last_one):
        @pl.loop(first, last_one)
        def _(e):
            @pl.when(has_up)
            def _():
                pl.when((e >= EARLY - 1) & (e < edges - 1))(lambda: up_message(0, e).start())
                up_message(1, e).start()

    @pl.when(depth == 0)
    def _():
        moist[0] = moist[0] + face_scale * rain[...]

    def face_step(e):
        where = pl.ds(pl.multiple_of(e * RE, RE), RE)

        @pl.when(has_down)
        def _():
            remote(up_pc.at[e], up_pc.at[e], face_send.at[2], up_recv.at[e], below).wait_recv()
            value = flux(pbuf[last, where, part_b], c7[where, part_b], up_pc[e, 0], up_pc[e, 1])
            fb_out[where] = value
            moist[last, where, part_b] = moist[last, where, part_b] - value
            flux_down(e).start()

        @pl.when(has_up)
        def _():
            for k in range(2):

                @pl.when(e == k * (edges // 2))
                def _():
                    where = pl.ds(k * half, half)
                    remote(dn_p.at[where], dn_p.at[where], face_send.at[0], down_recv.at[2 + k], above).wait_recv()
                    down_c(k).wait_recv()

            value = flux(dn_p[where], dn_c[where], pbuf[0, where, part_a], c0[where, part_a])
            fa_out[where] = value
            moist[0, where, part_a] = moist[0, where, part_a] + value
            flux_up(e).start()

    sub = lax.broadcasted_iota(jnp.int32, (8, wide), 0)

    def rows_of(t, count=1):
        return pl.ds(pl.multiple_of(8 * t, 8), 8 * count)

    def around(ref, q, t):
        north_t, a, b, south_t = (ref[q, rows_of(t + k), :] for k in (-1, 0, 1, 2))

        def sums(before, here, after):
            down = [pltpu.roll(v, 1, 0) for v in (before, here)]
            up = [pltpu.roll(v, 7, 0) for v in (here, after)]
            return (
                pltpu.roll(here, 1, 1)
                + pltpu.roll(here, wide - 1, 1)
                + jnp.where(sub == 0, down[0], down[1])
                + jnp.where(sub == 7, up[1], up[0])
            )

        return jnp.concatenate([sums(north_t, a, b), sums(a, b, south_t)], axis=0)

    def wave(j, stages):
        at = (2 * j + 2, 2 * j, 2 * j - 3, 2 * j - 6)
        out = []
        if 3 in stages:
            here = rows_of(at[3], 2)
            out.append((H, 2, here, A[2, here, :] + A[3, here, :] * around(H, 1, at[3])))
        if 2 in stages:
            here = rows_of(at[2], 2)
            out.append((H, 1, here, A[0, here, :] + A[1, here, :] * around(H, 0, at[2])))
        if 1 in stages:
            here = rows_of(at[1], 2)
            out.append((H, 0, here, A[0, here, :] + A[1, here, :] * around(E, 3, at[1])))
        if 0 in stages:
            here = rows_of(at[0], 2)
            root = E[0, here, :]
            scale = 1.0 / (E[1, here, :] + root * around(E, 0, at[0]))
            free, bound = E[2, here, :] * scale, root * scale
            out += [(A, 0, here, root * free), (A, 1, here, root * bound), (A, 2, here, free), (A, 3, here, bound)]
        for ref, q, here, value in out:
            ref[q, here, :] = value

    def head_copy(chunk, source):
        where = pl.ds(pl.multiple_of(chunk * R, R), R)
        return remote(
            heads.at[source, where], heads.at[source, where],
            head_send.at[0], head_recv.at[source], {"depth": 3},
        )

    def hand_on(chunk):
        where = pl.ds(pl.multiple_of(chunk * R, R), R)
        value = H[SWEEPS - 1, pl.ds(pl.multiple_of(PAD + chunk * R, 8), R), mid]
        heads[depth, where] = value
        head[where, :] = value
        pl.when(depth < 3)(lambda: head_copy(chunk, depth).start())

    await_announced()
    pl.when(has_north)(lambda: send_rows(0))
    pl.when(has_south)(lambda: send_rows(1))

    def posts(down, up):
        for copy in down:
            pl.when(has_down)(copy)
        post_faces(*up)

    pack(0)
    finish(1)
    finish(2)
    pack(1)
    finish(3)
    posts([lambda: down_c(0).start()], (0, 2))
    finish(4)
    pack(2)
    posts([lambda: down_p(EARLY - 1).start()], (2, 3))
    finish(5)
    pack(3)
    posts([lambda: down_c(1).start()], (3, 4))
    finish(6)

    pl.when(has_south)(lambda: take_rows(0))
    pl.when(has_north)(lambda: take_rows(1))
    pack(4)
    posts([lambda e=e: down_p(e).start() for e in range(EARLY, edges - 1)], (4, edges))
    face_step(0)
    face_step(1)

    for m in range(4):
        unpack(m)
    face_step(2)
    unpack(4)

    every = (0, 1, 2, 3)
    wave(0, (0,))
    wave(1, (0, 1))
    wave(2, (0, 1, 2))
    wave(3, (0, 1, 2))
    wave(4, (0, 1, 2, 3))
    face_step(3)

    @pl.loop(5, chunks - 1)
    def _(j):
        wave(j, every)
        hand_on(j - 5)

    face_step(4)

    @pl.loop(chunks - 1, chunks + 1)
    def _(j):
        wave(j, every)
        hand_on(j - 5)

    for j, stages in ((chunks + 1, (1, 2, 3)), (chunks + 2, (2, 3)), (chunks + 3, (2, 3)), (chunks + 4, (3,))):
        wave(j, stages)
        hand_on(j - 5)

    @pl.loop(5, edges)
    def _(e):
        face_step(e)

    @pl.when(depth == 3)
    def _():
        for block in range(4):
            if block < 3:
                remote(heads.at[block], heads.at[block], head_send.at[0], head_recv.at[block], {"depth": 0}).wait_recv()
            cols = pl.ds(block * tile, tile)
            bottom = c7[:, cols] * (
                (pbuf[last, :, cols] - heads[block]) * (2.0 * face_scale / layer_thick) + face_scale
            )
            moist[last, :, cols] = moist[last, :, cols] - bottom

    @pl.when(has_down)
    def _():
        remote(fa_in, fa_in, face_send.at[5], fa_recv.at[0], below).wait_recv()
        moist[last, :, part_a] = moist[last, :, part_a] - fa_in[...]

    @pl.when(has_up)
    def _():
        remote(fb_in, fb_in, face_send.at[4], fb_recv.at[0], above).wait_recv()
        moist[0, :, part_b] = moist[0, :, part_b] + fb_in[...]

    remote(part.at[:, 1 - core], recv1, s1_send.at[0], s1_recv.at[0], mate).wait_send()
    remote(xs, recv2, s2_send.at[0], s2_recv.at[0], cross).wait_send()

    @pl.when(has_down)
    def _():
        remote(c7.at[:, part_a], dn_p, face_send.at[0], down_recv.at[2], below).wait_send()
        remote(c7.at[:, part_a], dn_c, face_send.at[1], down_recv.at[1], below).wait_send()
        remote(fb_out, fb_in, face_send.at[4], fb_recv.at[0], below).wait_send()
        remote(colsend.at[0], colrecv.at[0], col_send.at[0], col_recv.at[0], below).wait_send()
        remote(heads.at[depth], heads.at[depth], head_send.at[0], head_recv.at[depth], {"depth": 3}).wait_send()

    @pl.when(has_up)
    def _():
        remote(c0.at[:, part_b], fb_in, face_send.at[2], up_recv.at[0], above).wait_send()
        remote(c0.at[:, part_b], fb_in, face_send.at[3], up_recv.at[0], above).wait_send()
        remote(fa_out, fa_in, face_send.at[5], fa_recv.at[0], above).wait_send()
        remote(colsend.at[1], colrecv.at[1], col_send.at[1], col_recv.at[0], above).wait_send()

    pl.when(has_north)(lambda: row_halo(0).wait_send())
    pl.when(has_south)(lambda: row_halo(1).wait_send())


def store_kernel(moist, head, moist_out, head_out, sems):
    copies = [pltpu.make_async_copy(head, head_out, sems.at[0])]
    for k in range(moist.shape[0]):
        copies.append(pltpu.make_async_copy(moist.at[k], moist_out.at[k], sems.at[k + 1]))
    for copy in copies:
        copy.start()
    for copy in copies:
        copy.wait()


def shards(strips, pressure, texture, active, rain, k_sat, alpha, theta_sat, head_old, cell_code, section):
    layers, rows, cols = pressure.shape
    tile = head_old.shape[1]
    wide = tile + LANES
    cols_a = 3 * LANES
    cols_b = cols - cols_a
    chunks, edges = rows // R, rows // RE
    f32 = jnp.float32
    vmem = lambda *shape: pltpu.VMEM(shape, f32)
    dma = lambda *shape: pltpu.SemaphoreType.DMA(shape)
    table = pltpu.SMEM(k_sat.shape, f32)
    scratch = [
        table,
        table,
        table,
        vmem(layers, rows, cols),
        pltpu.VMEM((layers, rows, cols), jnp.int32),
        pltpu.VMEM((layers, rows, cols), jnp.int32),
        vmem(rows, cols),
        vmem(rows, tile),
        pltpu.VMEM((rows, tile), jnp.int32),
        vmem(rows, tile),
        vmem(3, 2, 8, LANES),
        vmem(chunks, 2, 2, 3, R, tile),
        vmem(chunks, 2, 3, R, tile),
        vmem(chunks, 3, R, tile),
        vmem(chunks, 3, R, tile),
        vmem(rows, cols),
        vmem(rows, cols),
        vmem(rows, cols_a),
        vmem(rows, cols_a),
        vmem(edges, 2, RE, cols_b),
        vmem(rows, cols_b),
        vmem(rows, cols_b),
        vmem(rows, cols_a),
        vmem(rows, cols_a),
        vmem(4, rows + 2 * PAD, wide),
        vmem(SWEEPS, rows + 2 * PAD, wide),
        vmem(4, rows + 2 * PAD, wide),
        vmem(2, 5, 8, LANES),
        vmem(2, 5, 8, LANES),
        vmem(4, rows, tile),
        vmem(2, 8, 3 * LANES),
        vmem(2, 8, 3 * LANES),
        dma(chunks),
        dma(4),
        dma(1),
        dma(chunks),
        dma(1),
        dma(chunks),
        dma(6),
        dma(4),
        dma(edges),
        dma(1),
        dma(1),
        dma(2),
        dma(5),
        dma(2),
        dma(2),
        dma(1),
        dma(4),
        pltpu.SemaphoreType.REGULAR((3,)),
    ]
    anywhere = pl.BlockSpec(memory_space=pltpu.HBM)
    moist, head = pl.pallas_call(
        functools.partial(kernel, strips),
        out_shape=(
            pltpu.VMEM((layers, rows, cols), f32),
            pltpu.VMEM((rows, tile), f32),
        ),
        in_specs=[anywhere] * 10,
        out_specs=(pl.BlockSpec(memory_space=pltpu.VMEM), pl.BlockSpec(memory_space=pltpu.VMEM)),
        scratch_shapes=scratch,
        compiler_params=pltpu.CompilerParams(
            collective_id=0, has_side_effects=True, vmem_limit_bytes=59 * 2**20
        ),
        name="soil_column",
    )(k_sat, alpha, theta_sat, pressure, texture, active, rain, head_old, cell_code, section)
    on_chip = pl.BlockSpec(memory_space=pltpu.VMEM)
    return pl.pallas_call(
        store_kernel,
        out_shape=(
            jax.ShapeDtypeStruct((layers, rows, cols), f32),
            jax.ShapeDtypeStruct((rows, tile), f32),
        ),
        in_specs=[on_chip] * 2,
        out_specs=(anywhere, anywhere),
        scratch_shapes=[dma(layers + 1)],
        compiler_params=pltpu.CompilerParams(vmem_limit_bytes=2**20),
        name="store",
    )(pltpu.with_memory_space_constraint(moist, pltpu.VMEM), pltpu.with_memory_space_constraint(head, pltpu.VMEM))


def solution(mesh):
    in_specs = (
        P("depth", "strips", None),
        P("depth", "strips", None),
        P("depth", "strips", None),
        P("strips", None),
        P(),
        P(),
        P(),
        P("strips", "depth"),
        P("strips", "depth"),
        P("strips", "depth"),
    )
    out_specs = (P("depth", "strips", None), P("strips", "depth"))
    body = functools.partial(shards, mesh.shape["strips"])
    return jax.shard_map(body, mesh=mesh, in_specs=in_specs, out_specs=out_specs, check_vma=False)
```
